256 devices in a mesh: rows: 32 (over z, y), feat: 8 (over x, core).
Axes of the slice: x: 4, y: 4, z: 8, core: 2. Of those that a mesh axis runs over, the one named last changes fastest.
Arguments:
- gradient: float32 [524288], P('rows'), may hold values from -6 to 6
- hessian: bfloat16 [524288], P('rows'), may hold values from 0.049804688 to 1
- groups: int32 [524288], P('rows'), may hold values from 0 to 16383
- leaf_ids: int32 [524288], P('rows'), may hold values from 0 to 31
- bins: int32 [256, 524288], P('feat', 'rows'), may hold values from 0 to 63
- group_sizes: int32 [16384], P('rows'), may hold values from 16 to 63
- variance_ratio: float32 [1], replicated, may hold values from 1 to 16
Outputs:
- histograms: float32 [32, 256, 128], P('rows', 'feat')
- group_means: float32 [16384], P('rows')
The draws below stay inside these ranges and needn't reach their ends.
All inputs are finite; a program needn't handle non-finite values.
Results may differ from the reference program's by a relative error of at most 0.00038.
Values sent between devices are 32-bit elements; how exact they have to be, the bound alone decides.
A program may use at most 64 MiB of HBM per device.

```python
import math
import jax
import jax.numpy as jnp
import numpy as np
from jax import lax

F = 256
BINS = 64
LEAVES = 32
ROWS = 524288
GROUPS = 16384


def set_ends(drawn, key, low, high):
    longest = drawn.shape.index(max(drawn.shape))
    spots = []
    for shift in (0, 1):
        where = [jax.random.randint(jax.random.fold_in(key, axis), (), 0, length) for axis, length in enumerate(drawn.shape)]
        where[longest] = (where[longest] + shift) % drawn.shape[longest]
        spots.append(tuple(where))
    return drawn.at[spots[0]].set(low).at[spots[1]].set(high)


def block_scale(own_key, shape, pieces, low, top_value):
    level, own = 1.0, jax.random.fold_in(own_key, 6)
    for dim, parts in pieces:
        steps = jnp.exp(jax.random.uniform(jax.random.fold_in(own, dim), (parts,), jnp.float32, low / len(pieces), top_value / len(pieces)))
        level = level * jnp.repeat(steps, shape[dim] // parts).reshape([-1 if axis == dim else 1 for axis in range(len(shape))])
    return level


def rank_bounds(amount, lean):
    weights = [(1 << 20) // math.isqrt(grade ** lean) + 1 for grade in range(1, amount + 1)]
    deviation = 1 + sum(weights) // (1 << 30)
    return np.cumsum(np.array([max(1, weight // deviation) for weight in weights]))


def ranked_ids(rng, shape, count, slope):
    grid = rank_bounds(count, slope)
    ticket = jax.random.randint(jax.random.fold_in(rng, 1), shape, 0, int(grid[count - 1]))
    rank = jnp.searchsorted(jnp.asarray(grid, jnp.int32), ticket, side="right")
    return jax.random.permutation(jax.random.fold_in(rng, 2), count)[rank].astype(jnp.int32)


def bell_draw(own_key, shape, spread, most, cuts=(), kind=jnp.bfloat16):
    level = block_scale(own_key, shape, cuts, -0.22, 0.18) if cuts else 1.0
    drawn = jax.random.normal(own_key, shape, jnp.float32) * spread * level
    return jnp.minimum(jnp.maximum(drawn, -most), most).astype(kind)


def setup_inputs(seed: int = 0) -> dict:
    key_of = jax.random.split(jax.random.key(seed), 8)
    return {
        "gradient": bell_draw(key_of[0], (ROWS,), 1.0, 6.0, ((0, 32),), jnp.float32),
        "hessian": jnp.clip(0.049804688 + 0.9501953 * jax.random.uniform(key_of[1], (ROWS,), jnp.float32) ** block_scale(key_of[1], (ROWS,), ((0, 32),), -0.2, 0.2), 0.049804688, 1.0).astype(jnp.bfloat16),
        "groups": set_ends(ranked_ids(key_of[2], (ROWS,), GROUPS, 1), jax.random.fold_in(key_of[2], 3), 0, GROUPS - 1).astype(jnp.int32),
        "leaf_ids": set_ends(jax.random.randint(key_of[3], (ROWS,), 0, LEAVES), jax.random.fold_in(key_of[3], 1), 0, LEAVES - 1).astype(jnp.int32),
        "bins": set_ends(jax.random.randint(key_of[4], (F, ROWS), 0, BINS), jax.random.fold_in(key_of[4], 1), 0, BINS - 1).astype(jnp.int32),
        "group_sizes": set_ends(jax.random.randint(key_of[5], (GROUPS,), 16, 64), jax.random.fold_in(key_of[5], 1), 16, 63).astype(jnp.int32),
        "variance_ratio": jnp.clip(jnp.exp(jax.random.uniform(key_of[6], (1,), jnp.float32, math.log(1.0), math.log(16.0))), 1.0, 16.0),
    }


def reference(gradient, hessian, groups, leaf_ids, bins, group_sizes, variance_ratio):
    group_total = jax.ops.segment_sum(gradient, groups, num_segments=GROUPS)
    group_means = -group_total / (group_sizes.astype(jnp.float32) + variance_ratio[0])
    adjusted = (gradient + hessian.astype(jnp.float32) * group_means[groups]).astype(jnp.bfloat16)
    weights = jnp.stack([adjusted.astype(jnp.float32), hessian.astype(jnp.float32)], axis=1)

    def one_feature(column):
        index = (leaf_ids * BINS + column).astype(jnp.int32)
        return jax.ops.segment_sum(weights, index, num_segments=LEAVES * BINS)

    per_feature = lax.map(one_feature, bins)
    histograms = per_feature.reshape(F, LEAVES, BINS, 2).transpose(1, 0, 3, 2).reshape(LEAVES, F, 2 * BINS)
    return histograms, group_means
```

```python
import functools

import jax
import jax.numpy as jnp
from jax import lax
from jax.experimental import pallas as pl
from jax.experimental.pallas import tpu as pltpu
from jax.sharding import PartitionSpec as P

BINS = 64
LEAVES = 32
F8 = jnp.float8_e4m3fn
BF = jnp.bfloat16
F32 = jnp.float32
I32 = jnp.int32
MESH = pl.DeviceIdType.MESH
NT = (((1,), (1,)), ((), ()))
NY, NZ, NF = 4, 8, 8
LO, HI = 64, 256
CHUNKS = 4
PARTS = (20, 46, 64)


def iota0(dtype, rows, lanes):
    return lax.broadcasted_iota(I32, (rows, lanes), 0).astype(dtype)


def split(value, count):
    terms = []
    for _ in range(count):
        term = value.astype(BF).astype(F32)
        terms.append(term)
        value = value - term
    return terms


def kernel(
    g_ref, h_ref, group_ref, leaf_ref, size_ref, ratio_ref, bins_hbm,
    hist_ref, mean_ref,
    bins_ref, high_ref, hot_ref, left_ref,
    pay_ref, pay_in, mid_ref, mid_in, table_ref,
    out_y, in_y, out_z, in_z,
    bins_sem, ps, pr, ms, mr, ts, tr, ys, yr, zs, zr,
):
    rows, feat = lax.axis_index("rows"), lax.axis_index("feat")
    z, y = rows // NY, lax.rem(rows, NY)

    def y_peer(k):
        return (z * NY + lax.rem(y + k, NY), feat)

    def z_peer(k):
        return (lax.rem(z + k, NZ) * NY + y, feat)

    def f_peer(k):
        return (rows, lax.rem(feat + k, NF))

    def send(src, dst, send_sem, recv_sem, peer):
        return pltpu.make_async_remote_copy(
            src_ref=src, dst_ref=dst, send_sem=send_sem, recv_sem=recv_sem,
            device_id=peer, device_id_type=MESH,
        )

    fetch = pltpu.make_async_copy(bins_hbm, bins_ref, bins_sem)
    fetch.start()
    barrier = pltpu.get_barrier_semaphore()
    for peer in (
        [y_peer(k) for k in range(1, NY)]
        + [z_peer(k) for k in range(1, NZ)]
        + [f_peer(k) for k in range(1, NF)]
    ):
        pl.semaphore_signal(barrier, inc=1, device_id=peer, device_id_type=MESH)

    def hot_high(ids):
        wide = jnp.broadcast_to(ids // LO, (HI, 128)).astype(jnp.int16)
        return jnp.where(wide == iota0(jnp.int16, HI, 128), BF(1), BF(0))

    def low_rows(ids, values):
        own = jnp.broadcast_to(lax.rem(ids, LO) - 8 * feat, (8, 128)) == iota0(I32, 8, 128)
        return [jnp.where(own, jnp.broadcast_to(v, (8, 128)), 0.0) for v in values]

    def sum_step(t, total):
        left, right = [], []
        for u in range(4):
            row = pl.ds(4 * t + u, 1)
            ids = group_ref[row, :]
            hot = hot_high(ids)
            high_ref[:, pl.ds(pl.multiple_of(512 * t + 128 * u, 128), 128)] = hot
            right.append(hot)
            left.append(jnp.concatenate(low_rows(ids, split(g_ref[row, :], 3)), 0).astype(BF))
        return total + lax.dot_general(
            jnp.concatenate(left, 1), jnp.concatenate(right, 1), NT, preferred_element_type=F32
        )

    total = lax.fori_loop(0, 32, sum_step, jnp.zeros((24, HI), F32))
    pay_ref[0:8, :] = total[0:8] + total[8:16] + total[16:24]
    left, right = [], []
    for u in range(4):
        ids = 512 * rows + 128 * u + lax.broadcasted_iota(I32, (1, 128), 1)
        right.append(hot_high(ids))
        left.append(low_rows(ids, [size_ref[u : u + 1, :]])[0].astype(BF))
    pay_ref[8:16, :] = lax.dot_general(
        jnp.concatenate(left, 1), jnp.concatenate(right, 1), NT, preferred_element_type=F32
    )

    pl.semaphore_wait(barrier, NY + NZ + NF - 3)

    def hot_step(t, _):
        lanes = pl.ds(pl.multiple_of(256 * t, 256), 256)
        for f in range(32):
            wide = jnp.broadcast_to(bins_ref[f : f + 1, lanes], (BINS, 256)).astype(jnp.int8)
            hot_ref[BINS * f : BINS * (f + 1), lanes] = jnp.where(
                wide == iota0(jnp.int8, BINS, 256), F8(1), F8(0)
            )
        return 0

    def build(first, last):
        lax.fori_loop(first, last, hot_step, 0)

    copies = [
        send(pay_ref, pay_in.at[k - 1], ps.at[k - 1], pr.at[k - 1], y_peer(k))
        for k in range(1, NY)
    ]
    for copy in copies:
        copy.start()
    fetch.wait()
    build(0, PARTS[0])
    for copy in copies:
        copy.wait()
    mid_ref[...] = pay_ref[...] + pay_in[0] + pay_in[1] + pay_in[2]

    copies = [
        send(mid_ref, mid_in.at[k - 1], ms.at[k - 1], mr.at[k - 1], z_peer(k))
        for k in range(1, NZ)
    ]
    for copy in copies:
        copy.start()
    build(PARTS[0], PARTS[1])
    for copy in copies:
        copy.wait()
    total = mid_ref[...]
    for k in range(NZ - 1):
        total = total + mid_in[k]
    mine = pl.ds(pl.multiple_of(8 * feat, 8), 8)
    table_ref[mine, :] = -total[0:8] / (total[8:16] + ratio_ref[0])

    copies = [
        send(table_ref.at[mine], table_ref.at[mine], ts.at[k - 1], tr.at[k - 1], f_peer(k))
        for k in range(1, NF)
    ]
    for copy in copies:
        copy.start()
    build(PARTS[1], PARTS[2])
    for copy in copies:
        copy.wait()

    table = table_ref[...]
    terms = split(table, 3)
    wanted = lax.broadcasted_iota(I32, (8, HI), 1) - 8 * rows
    line = lax.broadcasted_iota(I32, (8, HI), 0)
    halves = []
    for half in range(2):
        pick = jnp.where(wanted == 2 * line + half, 1.0, 0.0).astype(BF)
        halves.append(
            sum(
                lax.dot_general(pick, term.astype(BF), NT, preferred_element_type=F32)
                for term in terms
            )
        )
    mean_ref[...] = jnp.concatenate(halves, 1)[0:4]
    bound = jnp.max(jnp.max(jnp.abs(table), axis=0, keepdims=True), axis=1, keepdims=True) + 6.0
    left_over = bound * 2.0**60
    scale = jnp.full_like(bound, 2.0**60)
    for step in (64, 32, 16, 8, 4, 2, 1):
        large = left_over >= 2.0**step
        left_over = jnp.where(large, left_over * 2.0**-step, left_over)
        scale = jnp.where(large, scale * 2.0**-step, scale)
    back = jnp.full_like(scale, 2.0**-7) / scale
    scale = scale * 2.0**7
    table2 = jnp.concatenate(terms[0:2], 0).astype(BF)

    def left_step(t, _):
        lanes = pl.ds(pl.multiple_of(256 * t, 256), 256)
        found = jnp.dot(table2, high_ref[:, lanes], preferred_element_type=F32)
        found = found[0:LO] + found[LO : 2 * LO]
        for u in range(2):
            row = pl.ds(2 * t + u, 1)
            part = found[:, 128 * u : 128 * (u + 1)]
            low = jnp.broadcast_to(lax.rem(group_ref[row, :], LO), (LO, 128))
            part = jnp.where(low == iota0(I32, LO, 128), part, 0.0)
            mean = jnp.sum(part, axis=0, keepdims=True)
            hess = h_ref[row, :]
            adjusted = (g_ref[row, :] + hess * mean).astype(BF).astype(F32) * scale
            hess = hess * 128.0
            leaf = leaf_ref[row, :]
            place = lax.rem(leaf, NY) * NZ + leaf // NY
            wide = jnp.broadcast_to(place, (LEAVES, 128)).astype(jnp.int8)
            member = wide == iota0(jnp.int8, LEAVES, 128)
            at = pl.ds(pl.multiple_of(256 * t + 128 * u, 128), 128)
            for c, value in enumerate((adjusted, hess)):
                first = value.astype(F8)
                second = ((value - first.astype(F32)) * 16.0).astype(F8).astype(F32)
                for p, term in enumerate((first.astype(F32), second)):
                    term = jnp.broadcast_to(term, (LEAVES, 128)).astype(F8)
                    begin = LEAVES * (2 * c + p)
                    left_ref[begin : begin + LEAVES, at] = jnp.where(member, term, F8(0))
        return 0

    lax.fori_loop(0, 64, left_step, 0)

    low_half = lax.broadcasted_iota(I32, (8, 128), 1) < BINS

    def histogram(c):
        def step(n, _):
            block = 2 * c + n
            hot = hot_ref[pl.ds(pl.multiple_of(256 * block, 256), 256), :]
            both = lax.dot_general(left_ref[...], hot, NT, preferred_element_type=F32)
            grad = (both[0:32] + both[32:64] * 0.0625) * back
            hess = (both[64:96] + both[96:128] * 0.0625) * (1.0 / 128.0)
            for to in range(NY):
                for pair in range(2):
                    a = grad[8 * to : 8 * to + 8, 128 * pair : 128 * pair + 128]
                    b = hess[8 * to : 8 * to + 8, 128 * pair : 128 * pair + 128]
                    out_y[c, to, 4 * n + 2 * pair] = jnp.where(low_half, a, pltpu.roll(b, 64, 1))
                    out_y[c, to, 4 * n + 2 * pair + 1] = jnp.where(low_half, pltpu.roll(a, 64, 1), b)
            return 0

        lax.fori_loop(0, 2, step, 0)

    def y_copies(c):
        return [
            send(
                out_y.at[c, lax.rem(y + k, NY)], in_y.at[c, k - 1],
                ys.at[c, k - 1], yr.at[c, k - 1], y_peer(k),
            )
            for k in range(1, NY)
        ]

    def z_copies(c):
        return [
            send(
                out_z.at[c, pl.ds(pl.multiple_of(8 * lax.rem(z + k, NZ), 8), 8)],
                in_z.at[c, k - 1], zs.at[c, k - 1], zr.at[c, k - 1], z_peer(k),
            )
            for k in range(1, NZ)
        ]

    def second_stage(c):
        for copy in y_copies(c):
            copy.wait()
        for f in range(8):
            part = out_y[c, y, f] + in_y[c, 0, f] + in_y[c, 1, f] + in_y[c, 2, f]
            out_z[c, pl.ds(f, 8, stride=8), :] = part
        for copy in z_copies(c):
            copy.start()

    def finish(c):
        for copy in z_copies(c):
            copy.wait()
        part = out_z[c, pl.ds(pl.multiple_of(8 * z, 8), 8), :]
        for k in range(NZ - 1):
            part = part + in_z[c, k]
        hist_ref[8 * c : 8 * c + 8, :] = part

    for c in range(CHUNKS):
        histogram(c)
        for copy in y_copies(c):
            copy.start()
        if c >= 2:
            second_stage(c - 2)
    second_stage(CHUNKS - 2)
    second_stage(CHUNKS - 1)
    for c in range(CHUNKS):
        finish(c)


def shards(gradient, hessian, groups, leaf_ids, bins, group_sizes, variance_ratio):
    count = gradient.shape[0]
    vmem, sem = pltpu.VMEM, pltpu.SemaphoreType.DMA
    whole = pl.BlockSpec(memory_space=pltpu.VMEM)
    hist, means = pl.pallas_call(
        kernel,
        out_shape=(jax.ShapeDtypeStruct((32, 128), F32), jax.ShapeDtypeStruct((4, 128), F32)),
        in_specs=[whole] * 5
        + [pl.BlockSpec(memory_space=pltpu.SMEM), pl.BlockSpec(memory_space=pl.ANY)],
        out_specs=(whole, whole),
        scratch_shapes=[
            vmem((32, count), I32),
            vmem((HI, count), BF),
            vmem((32 * BINS, count), F8),
            vmem((4 * LEAVES, count), F8),
            vmem((16, HI), F32),
            vmem((NY - 1, 16, HI), F32),
            vmem((16, HI), F32),
            vmem((NZ - 1, 16, HI), F32),
            vmem((LO, HI), F32),
            vmem((CHUNKS, NY, 8, 8, 128), F32),
            vmem((CHUNKS, NY - 1, 8, 8, 128), F32),
            vmem((CHUNKS, 64, 128), F32),
            vmem((CHUNKS, NZ - 1, 8, 128), F32),
            sem,
            sem((NY - 1,)), sem((NY - 1,)),
            sem((NZ - 1,)), sem((NZ - 1,)),
            sem((NF - 1,)), sem((NF - 1,)),
            sem((CHUNKS, NY - 1)), sem((CHUNKS, NY - 1)),
            sem((CHUNKS, NZ - 1)), sem((CHUNKS, NZ - 1)),
        ],
        compiler_params=pltpu.CompilerParams(
            collective_id=0, has_side_effects=True, vmem_limit_bytes=62 * 1024 * 1024
        ),
    )(
        gradient.reshape(128, 128),
        hessian.astype(F32).reshape(128, 128),
        groups.reshape(128, 128),
        leaf_ids.reshape(128, 128),
        group_sizes.astype(F32).reshape(4, 128),
        variance_ratio,
        bins,
    )
    return hist.reshape(1, 32, 128), means.reshape(512)


def solution(mesh):
    in_specs = (P("rows"), P("rows"), P("rows"), P("rows"), P("feat", "rows"), P("rows"), P())
    out_specs = (P("rows", "feat", None), P("rows"))
    return jax.shard_map(shards, mesh=mesh, in_specs=in_specs, out_specs=out_specs, check_vma=False)
```

```python
import functools

import jax
import jax.numpy as jnp
from jax import lax
from jax.experimental import pallas as pl
from jax.experimental.pallas import tpu as pltpu
from jax.sharding import PartitionSpec as P

BINS = 64
LEAVES = 32
F8 = jnp.float8_e4m3fn
BF = jnp.bfloat16
F32 = jnp.float32
I32 = jnp.int32
MESH = pl.DeviceIdType.MESH
NT = (((1,), (1,)), ((), ()))
NY, NZ, NF = 4, 8, 8
BLOCKS = 4
CHUNKS = 4
PARTS = (20, 46, 64)


def iota0(dtype, rows, lanes):
    return lax.broadcasted_iota(I32, (rows, lanes), 0).astype(dtype)


def split(value, count):
    terms = []
    for _ in range(count):
        term = value.astype(BF).astype(F32)
        terms.append(term)
        value = value - term
    return terms


def kernel(
    g_ref, h_ref, group_ref, leaf_ref, size_ref, ratio_ref, bins_hbm,
    hist_ref, mean_ref,
    bins_ref, hot_ref, left_ref, low_hot_ref,
    ids_ref, term_ref, row_mean_ref,
    pay_ref, pay_in, mid_ref, mid_in, own_size_ref, size_y_ref, size_z_ref, size_in_ref, table_ref,
    out_y, in_y, out_z, in_z,
    bins_sem, ps, pr, ms, mr, ts, tr, ss, sr, us, ur, ys, yr, zs, zr,
):
    rows, feat = lax.axis_index("rows"), lax.axis_index("feat")
    z, y = rows // NY, lax.rem(rows, NY)

    def y_peer(k):
        return (z * NY + lax.rem(y + k, NY), feat)

    def z_peer(k):
        return (lax.rem(z + k, NZ) * NY + y, feat)

    def f_peer(k):
        return (rows, lax.rem(feat + k, NF))

    def send(src, dst, send_sem, recv_sem, peer):
        return pltpu.make_async_remote_copy(
            src_ref=src, dst_ref=dst, send_sem=send_sem, recv_sem=recv_sem,
            device_id=peer, device_id_type=MESH,
        )

    barrier = pltpu.get_barrier_semaphore()
    for peer in (
        [y_peer(k) for k in range(1, NY)]
        + [z_peer(k) for k in range(1, NZ)]
        + [f_peer(k) for k in range(1, NF)]
    ):
        pl.semaphore_signal(barrier, inc=1, device_id=peer, device_id_type=MESH)
    fetch = pltpu.make_async_copy(bins_hbm, bins_ref, bins_sem)
    fetch.start()

    ids = group_ref[...]
    high, low = lax.shift_right_logical(ids, 7), ids & 127
    ids_ref[0] = high - 16 * feat
    ids_ref[1] = low
    ids_ref[2] = low + 2 * (high & 64)
    ids_ref[3] = high & 63
    leaf = leaf_ref[...]
    ids_ref[4] = (leaf & (NY - 1)) * NZ + lax.shift_right_logical(leaf, 2)
    for n, term in enumerate(split(g_ref[...], 3)):
        term_ref[n] = term
    left, right = [], []
    for t in range(128):
        row = slice(t, t + 1)
        wide = jnp.broadcast_to(ids_ref[1, row, :], (128, 128)).astype(jnp.int16)
        right.append(jnp.where(wide == iota0(jnp.int16, 128, 128), BF(1), BF(0)))
        wide = jnp.broadcast_to(ids_ref[0, row, :], (16, 128)).astype(jnp.int16)
        own = wide == iota0(jnp.int16, 16, 128)
        values = [
            jnp.where(own, jnp.broadcast_to(term_ref[n, row, :], (16, 128)).astype(BF), BF(0))
            for n in range(3)
        ]
        left.append(jnp.concatenate(values, 0))
    total = lax.dot_general(
        jnp.concatenate(left, 1), jnp.concatenate(right, 1), NT, preferred_element_type=F32
    )
    pay_ref[...] = total[0:16] + total[16:32] + total[32:48]
    own_size_ref[...] = size_ref[...].astype(F32)

    with jax.named_scope("bar"):
        pl.semaphore_wait(barrier, NY + NZ + NF - 3)

    def hot_step(t, _):
        lanes = pl.ds(pl.multiple_of(256 * t, 256), 256)
        for f in range(32):
            wide = jnp.broadcast_to(bins_ref[f : f + 1, lanes], (BINS, 256)).astype(jnp.int8)
            hot_ref[BINS * f : BINS * (f + 1), lanes] = jnp.where(
                wide == iota0(jnp.int8, BINS, 256), F8(1), F8(0)
            )
        return 0

    def build(first, last):
        with jax.named_scope("build"):
            lax.fori_loop(first, last, hot_step, 0)

    def left_rows(parts):
        def step(t, _):
            for u in range(16):
                row = pl.ds(16 * t + u, 1)
                wide = jnp.broadcast_to(ids_ref[4, row, :], (LEAVES, 128)).astype(jnp.int8)
                member = wide == iota0(jnp.int8, LEAVES, 128)
                at = pl.ds(pl.multiple_of(2048 * t + 128 * u, 128), 128)
                for c in parts:
                    term = jnp.broadcast_to(term_ref[c, row, :], (LEAVES, 128)).astype(F8)
                    left_ref[LEAVES * c : LEAVES * (c + 1), at] = jnp.where(member, term, F8(0))
            return 0

        with jax.named_scope("left"):
            lax.fori_loop(0, 8, step, 0)

    def left_terms(c, value):
        first = value.astype(F8).astype(F32)
        term_ref[c] = first
        term_ref[c + 1] = ((value - first) * 16.0).astype(F8).astype(F32)

    copies = [
        send(pay_ref, pay_in.at[k - 1], ps.at[k - 1], pr.at[k - 1], y_peer(k))
        for k in range(1, NY)
    ]
    for copy in copies:
        copy.start()
    sizes = [
        send(own_size_ref, size_y_ref.at[y], ss.at[k - 1], sr.at[k - 1], y_peer(k))
        for k in range(1, NY)
    ]
    for copy in sizes:
        copy.start()
    with jax.named_scope("fetch"):
        fetch.wait()
    build(0, PARTS[0])
    with jax.named_scope("cwait"):
        for copy in copies:
            copy.wait()
    mid_ref[...] = pay_ref[...] + pay_in[0] + pay_in[1] + pay_in[2]

    copies = [
        send(mid_ref, mid_in.at[k - 1], ms.at[k - 1], mr.at[k - 1], z_peer(k))
        for k in range(1, NZ)
    ]
    for copy in copies:
        copy.start()
    for copy in sizes:
        copy.wait()
    size_y_ref[y] = own_size_ref[...]
    for k in range(NY):
        size_z_ref[4 * k : 4 * k + 4, :] = size_y_ref[k]

    def size_copies():
        return [
            send(size_z_ref, size_in_ref, us.at[k - 1], ur, z_peer(k)) for k in range(1, NZ)
        ]

    @pl.when(z == feat)
    def _():
        for copy in size_copies():
            copy.start()

    build(PARTS[0], PARTS[1])

    def low_hot_step(t, _):
        for u in range(4):
            wide = jnp.broadcast_to(ids_ref[2, pl.ds(4 * t + u, 1), :], (256, 128))
            at = pl.ds(pl.multiple_of(512 * t + 128 * u, 128), 128)
            low_hot_ref[:, at] = jnp.where(
                wide.astype(jnp.int16) == iota0(jnp.int16, 256, 128), BF(1), BF(0)
            )
        return 0

    with jax.named_scope("lowhot"):
        lax.fori_loop(0, 32, low_hot_step, 0)
    hess = h_ref[...].astype(F32)
    left_terms(2, hess * 128.0)
    left_rows((2, 3))
    with jax.named_scope("cwait"):
        for copy in copies:
            copy.wait()
    @pl.when(z == feat)
    def _():
        for copy in size_copies():
            copy.wait_send()
        size_in_ref[...] = size_z_ref[...]

    @pl.when(z != feat)
    def _():
        size_copies()[0].wait_recv()
    total = mid_ref[...]
    for k in range(NZ - 1):
        total = total + mid_in[k]
    mine = pl.ds(pl.multiple_of(16 * feat, 16), 16)
    table_ref[mine, :] = -total / (size_in_ref[...] + ratio_ref[0])

    copies = [
        send(table_ref.at[mine], table_ref.at[mine], ts.at[k - 1], tr.at[k - 1], f_peer(k))
        for k in range(1, NF)
    ]
    for copy in copies:
        copy.start()
    build(PARTS[1], PARTS[2])
    with jax.named_scope("cwait"):
        for copy in copies:
            copy.wait()

    table = table_ref[...]
    mean_ref[...] = table_ref[pl.ds(pl.multiple_of(4 * rows, 4), 4), :]
    wide = jnp.concatenate([table[0:64], table[64:128]], 1)
    wide = jnp.concatenate(split(wide, 2), 0).astype(BF)
    with jax.named_scope("look"):
        for block in range(BLOCKS):
            span = 16384 // BLOCKS
            found = jnp.dot(
                wide, low_hot_ref[:, span * block : span * (block + 1)], preferred_element_type=F32
            )
            for u in range(span // 128):
                row = slice(block * (span // 128) + u, block * (span // 128) + u + 1)
                at = slice(128 * u, 128 * u + 128)
                part = found[0:64, at] + found[64:128, at]
                own = jnp.broadcast_to(ids_ref[3, row, :], (64, 128)) == iota0(I32, 64, 128)
                row_mean_ref[row, :] = jnp.sum(jnp.where(own, part, 0.0), axis=0, keepdims=True)
    bound = jnp.max(jnp.max(jnp.abs(table), axis=0, keepdims=True), axis=1, keepdims=True) + 6.0
    left_over = bound * 2.0**60
    scale = jnp.full_like(bound, 2.0**60)
    for step in (64, 32, 16, 8, 4, 2, 1):
        large = left_over >= 2.0**step
        left_over = jnp.where(large, left_over * 2.0**-step, left_over)
        scale = jnp.where(large, scale * 2.0**-step, scale)
    back = jnp.full_like(scale, 2.0**-7) / scale
    scale = scale * 2.0**7
    adjusted = (g_ref[...] + hess * row_mean_ref[...]).astype(BF).astype(F32)
    left_terms(0, adjusted * scale)
    left_rows((0, 1))

    low_half = lax.broadcasted_iota(I32, (8, 128), 1) < BINS

    def histogram(c):
        def step(n, _):
            block = 2 * c + n
            hot = hot_ref[pl.ds(pl.multiple_of(256 * block, 256), 256), :]
            both = lax.dot_general(left_ref[...], hot, NT, preferred_element_type=F32)
            grad = (both[0:32] + both[32:64] * 0.0625) * back
            hess = (both[64:96] + both[96:128] * 0.0625) * (1.0 / 128.0)
            for to in range(NY):
                for pair in range(2):
                    a = grad[8 * to : 8 * to + 8, 128 * pair : 128 * pair + 128]
                    b = hess[8 * to : 8 * to + 8, 128 * pair : 128 * pair + 128]
                    out_y[c, to, 4 * n + 2 * pair] = jnp.where(low_half, a, pltpu.roll(b, 64, 1))
                    out_y[c, to, 4 * n + 2 * pair + 1] = jnp.where(low_half, pltpu.roll(a, 64, 1), b)
            return 0

        with jax.named_scope("mm"):
            lax.fori_loop(0, 2, step, 0)

    def y_copies(c):
        return [
            send(
                out_y.at[c, lax.rem(y + k, NY)], in_y.at[c, k - 1],
                ys.at[c, k - 1], yr.at[c, k - 1], y_peer(k),
            )
            for k in range(1, NY)
        ]

    def z_copies(c):
        return [
            send(
                out_z.at[c, pl.ds(pl.multiple_of(8 * lax.rem(z + k, NZ), 8), 8)],
                in_z.at[c, k - 1], zs.at[c, k - 1], zr.at[c, k - 1], z_peer(k),
            )
            for k in range(1, NZ)
        ]

    def second_stage(c):
        with jax.named_scope("ywait"):
            for copy in y_copies(c):
                copy.wait()
        for f in range(8):
            part = out_y[c, y, f] + in_y[c, 0, f] + in_y[c, 1, f] + in_y[c, 2, f]
            out_z[c, pl.ds(f, 8, stride=8), :] = part
        for copy in z_copies(c):
            copy.start()

    def finish(c):
        with jax.named_scope("zwait"):
            for copy in z_copies(c):
                copy.wait()
        part = out_z[c, pl.ds(pl.multiple_of(8 * z, 8), 8), :]
        for k in range(NZ - 1):
            part = part + in_z[c, k]
        hist_ref[8 * c : 8 * c + 8, :] = part

    for c in range(CHUNKS):
        histogram(c)
        for copy in y_copies(c):
            copy.start()
        if c >= 2:
            second_stage(c - 2)
    second_stage(CHUNKS - 2)
    second_stage(CHUNKS - 1)
    for c in range(CHUNKS):
        finish(c)


def shards(gradient, hessian, groups, leaf_ids, bins, group_sizes, variance_ratio):
    count = gradient.shape[0]
    vmem, sem = pltpu.VMEM, pltpu.SemaphoreType.DMA
    whole = pl.BlockSpec(memory_space=pltpu.VMEM)
    hist, means = pl.pallas_call(
        kernel,
        out_shape=(jax.ShapeDtypeStruct((32, 128), F32), jax.ShapeDtypeStruct((4, 128), F32)),
        in_specs=[whole] * 5
        + [pl.BlockSpec(memory_space=pltpu.SMEM), pl.BlockSpec(memory_space=pl.ANY)],
        out_specs=(whole, whole),
        scratch_shapes=[
            vmem((32, count), I32),
            vmem((32 * BINS, count), F8),
            vmem((4 * LEAVES, count), F8),
            vmem((256, count), BF),
            vmem((5, 128, 128), I32),
            vmem((4, 128, 128), F32),
            vmem((128, 128), F32),
            vmem((16, 128), F32),
            vmem((NY - 1, 16, 128), F32),
            vmem((16, 128), F32),
            vmem((NZ - 1, 16, 128), F32),
            vmem((4, 128), F32),
            vmem((NY, 4, 128), F32),
            vmem((16, 128), F32),
            vmem((16, 128), F32),
            vmem((128, 128), F32),
            vmem((CHUNKS, NY, 8, 8, 128), F32),
            vmem((CHUNKS, NY - 1, 8, 8, 128), F32),
            vmem((CHUNKS, 64, 128), F32),
            vmem((CHUNKS, NZ - 1, 8, 128), F32),
            sem,
            sem((NY - 1,)), sem((NY - 1,)),
            sem((NZ - 1,)), sem((NZ - 1,)),
            sem((NF - 1,)), sem((NF - 1,)),
            sem((NY - 1,)), sem((NY - 1,)),
            sem((NZ - 1,)), sem,
            sem((CHUNKS, NY - 1)), sem((CHUNKS, NY - 1)),
            sem((CHUNKS, NZ - 1)), sem((CHUNKS, NZ - 1)),
        ],
        compiler_params=pltpu.CompilerParams(
            collective_id=0, has_side_effects=True, vmem_limit_bytes=56 * 1024 * 1024
        ),
    )(
        gradient.reshape(128, 128),
        hessian.reshape(128, 128),
        groups.reshape(128, 128),
        leaf_ids.reshape(128, 128),
        group_sizes.reshape(4, 128),
        variance_ratio,
        bins,
    )
    return hist.reshape(1, 32, 128), means.reshape(512)


def solution(mesh):
    in_specs = (P("rows"), P("rows"), P("rows"), P("rows"), P("feat", "rows"), P("rows"), P())
    out_specs = (P("rows", "feat", None), P("rows"))
    return jax.shard_map(shards, mesh=mesh, in_specs=in_specs, out_specs=out_specs, check_vma=False)
```

```python
import functools

import jax
import jax.numpy as jnp
from jax import lax
from jax.experimental import pallas as pl
from jax.experimental.pallas import tpu as pltpu
from jax.sharding import PartitionSpec as P

BINS = 64
LEAVES = 32
F8 = jnp.float8_e4m3fn
BF = jnp.bfloat16
F32 = jnp.float32
I32 = jnp.int32
MESH = pl.DeviceIdType.MESH
NT = (((1,), (1,)), ((), ()))
NY, NZ, NF = 4, 8, 8
BLOCKS = 2
SUM_ROWS = 64
CHUNKS = 4
PARTS = (4, 46, 64)


def iota0(dtype, rows, lanes):
    return lax.broadcasted_iota(I32, (rows, lanes), 0).astype(dtype)


def split(value, count):
    terms = []
    for _ in range(count):
        term = value.astype(BF).astype(F32)
        terms.append(term)
        value = value - term
    return terms


def kernel(
    g_ref, h_ref, group_ref, leaf_ref, size_ref, ratio_ref, bins_hbm,
    parts_ref, mean_ref,
    bins_ref, hot_ref, left_ref, low_hot_ref,
    ids_ref, term_ref, row_mean_ref,
    pay_ref, pay_in, mid_ref, mid_in, own_size_ref, size_in_y, size_z_ref, size_in_ref, table_ref,
    out_y, in_y, out_z,
    bins_sem, mean_sem, own_sem, send_sem, recv_sem, y_send, y_recv, z_send, z_recv,
):
    rows, feat = lax.axis_index("rows"), lax.axis_index("feat")
    z, y = rows // NY, lax.rem(rows, NY)

    def y_peer(k):
        return (z * NY + lax.rem(y + k, NY), feat)

    def z_peer(k):
        return (lax.rem(z + k, NZ) * NY + y, feat)

    def f_peer(k):
        return (rows, lax.rem(feat + k, NF))

    def send(src, dst, sems, peer):
        return pltpu.make_async_remote_copy(
            src_ref=src, dst_ref=dst, send_sem=sems[0], recv_sem=sems[1],
            device_id=peer, device_id_type=MESH,
        )

    def wait(ref, sem):
        pltpu.make_async_copy(ref, ref, sem).wait()

    def wait_both(ref, sems):
        for sem in sems:
            wait(ref, sem)

    pay_sems, size_sems, mid_sems, far_sems, table_sems = [
        (send_sem.at[n], recv_sem.at[n]) for n in range(5)
    ]

    barrier = pltpu.get_barrier_semaphore()
    for peer in (
        [y_peer(k) for k in range(1, NY)]
        + [z_peer(k) for k in range(1, NZ)]
        + [f_peer(k) for k in range(1, NF)]
    ):
        pl.semaphore_signal(barrier, inc=1, device_id=peer, device_id_type=MESH)
    fetch = pltpu.make_async_copy(bins_hbm, bins_ref, bins_sem)
    fetch.start()

    ids = group_ref[...]
    high, low = lax.shift_right_logical(ids, 7), ids & 127
    ids_ref[0] = high - 16 * feat
    ids_ref[1] = low
    ids_ref[2] = low + 2 * (high & 64)
    ids_ref[3] = high & 63
    leaf = leaf_ref[...]
    ids_ref[4] = (leaf & (NY - 1)) * NZ + lax.shift_right_logical(leaf, 2)
    for n, term in enumerate(split(g_ref[...], 3)):
        term_ref[n] = term

    def sum_step(n, total):
        left, right = [], []
        for t in range(SUM_ROWS):
            row = pl.ds(SUM_ROWS * n + t, 1)
            wide = jnp.broadcast_to(ids_ref[1, row, :], (128, 128)).astype(jnp.int16)
            right.append(jnp.where(wide == iota0(jnp.int16, 128, 128), BF(1), BF(0)))
            wide = jnp.broadcast_to(ids_ref[0, row, :], (16, 128)).astype(jnp.int16)
            own = wide == iota0(jnp.int16, 16, 128)
            values = [
                jnp.where(own, jnp.broadcast_to(term_ref[n, row, :], (16, 128)).astype(BF), BF(0))
                for n in range(3)
            ]
            left.append(jnp.concatenate(values, 0))
        return total + lax.dot_general(
            jnp.concatenate(left, 1), jnp.concatenate(right, 1), NT, preferred_element_type=F32
        )

    with jax.named_scope("gsum"):
        total = lax.fori_loop(0, 128 // SUM_ROWS, sum_step, jnp.zeros((48, 128), F32))
        pay_ref[...] = total[0:16] + total[16:32] + total[32:48]
    own_size_ref[...] = size_ref[...].astype(F32)

    with jax.named_scope("bar"):
        pl.semaphore_wait(barrier, NY + NZ + NF - 3)

    def hot_step(t, _):
        lanes = pl.ds(pl.multiple_of(256 * t, 256), 256)
        for f in range(32):
            wide = jnp.broadcast_to(bins_ref[f : f + 1, lanes], (BINS, 256)).astype(jnp.int8)
            hot_ref[BINS * f : BINS * (f + 1), lanes] = jnp.where(
                wide == iota0(jnp.int8, BINS, 256), F8(1), F8(0)
            )
        return 0

    def build(first, last):
        with jax.named_scope("build"):
            lax.fori_loop(first, last, hot_step, 0)

    def left_rows(parts):
        def step(t, _):
            for u in range(16):
                row = pl.ds(16 * t + u, 1)
                wide = jnp.broadcast_to(ids_ref[4, row, :], (LEAVES, 128)).astype(jnp.int8)
                member = wide == iota0(jnp.int8, LEAVES, 128)
                at = pl.ds(pl.multiple_of(2048 * t + 128 * u, 128), 128)
                for c in parts:
                    term = jnp.broadcast_to(term_ref[c, row, :], (LEAVES, 128)).astype(F8)
                    left_ref[LEAVES * c : LEAVES * (c + 1), at] = jnp.where(member, term, F8(0))
            return 0

        with jax.named_scope("left"):
            lax.fori_loop(0, 8, step, 0)

    def left_terms(c, value):
        first = value.astype(F8).astype(F32)
        term_ref[c] = first
        term_ref[c + 1] = ((value - first) * 16.0).astype(F8).astype(F32)

    for k in range(1, NY):
        send(pay_ref, pay_in.at[k - 1], pay_sems, y_peer(k)).start()
    for k in range(1, NY):
        send(own_size_ref, size_in_y.at[k - 1], size_sems, y_peer(k)).start()
    def low_hot_step(t, _):
        for u in range(4):
            wide = jnp.broadcast_to(ids_ref[2, pl.ds(4 * t + u, 1), :], (256, 128))
            at = pl.ds(pl.multiple_of(512 * t + 128 * u, 128), 128)
            low_hot_ref[:, at] = jnp.where(
                wide.astype(jnp.int16) == iota0(jnp.int16, 256, 128), BF(1), BF(0)
            )
        return 0

    with jax.named_scope("lowhot"):
        lax.fori_loop(0, 32, low_hot_step, 0)
    hess = h_ref[...].astype(F32)
    left_terms(2, hess * 128.0)
    left_rows((2, 3))
    with jax.named_scope("fetch"):
        fetch.wait()
    build(0, PARTS[0])
    with jax.named_scope("cwait"):
        wait_both(pay_in, pay_sems)
    mid_ref[...] = pay_ref[...] + pay_in[0] + pay_in[1] + pay_in[2]

    for k in range(1, NZ):
        send(mid_ref, mid_in.at[k - 1], mid_sems, z_peer(k)).start()
    wait_both(size_in_y, size_sems)
    size_z_ref[pl.ds(pl.multiple_of(4 * y, 4), 4), :] = own_size_ref[...]
    for k in range(1, NY):
        at = pl.ds(pl.multiple_of(4 * lax.rem(y + NY - k, NY), 4), 4)
        size_z_ref[at, :] = size_in_y[k - 1]

    @pl.when(z == feat)
    def _():
        for k in range(1, NZ):
            send(size_z_ref, size_in_ref, far_sems, z_peer(k)).start()

    build(PARTS[0], PARTS[1])

    with jax.named_scope("cwait"):
        wait_both(mid_in, mid_sems)

    @pl.when(z == feat)
    def _():
        wait(mid_in, far_sems[0])
        size_in_ref[...] = size_z_ref[...]

    @pl.when(z != feat)
    def _():
        wait(size_in_ref, far_sems[1])

    total = mid_ref[...]
    for k in range(NZ - 1):
        total = total + mid_in[k]
    mine = pl.ds(pl.multiple_of(16 * feat, 16), 16)
    table_ref[mine, :] = -total / (size_in_ref[...] + ratio_ref[0])

    for k in range(1, NF):
        send(table_ref.at[mine], table_ref.at[mine], table_sems, f_peer(k)).start()
    build(PARTS[1], PARTS[2])
    with jax.named_scope("cwait"):
        wait_both(table_ref.at[pl.ds(0, 16 * (NF - 1))], table_sems)

    table = table_ref[...]
    put_means = pltpu.make_async_copy(
        table_ref.at[pl.ds(pl.multiple_of(4 * rows, 4), 4)], mean_ref, mean_sem
    )
    put_means.start()
    wide = jnp.concatenate([table[0:64], table[64:128]], 1)
    wide = jnp.concatenate(split(wide, 2), 0).astype(BF)
    def look_step(block, _):
        span = 16384 // BLOCKS
        lanes = pl.ds(pl.multiple_of(span * block, span), span)
        found = jnp.dot(wide, low_hot_ref[:, lanes], preferred_element_type=F32)
        for u in range(span // 128):
            row = pl.ds(block * (span // 128) + u, 1)
            at = slice(128 * u, 128 * u + 128)
            part = found[0:64, at] + found[64:128, at]
            own = jnp.broadcast_to(ids_ref[3, row, :], (64, 128)) == iota0(I32, 64, 128)
            row_mean_ref[row, :] = jnp.sum(jnp.where(own, part, 0.0), axis=0, keepdims=True)
        return 0

    with jax.named_scope("look"):
        lax.fori_loop(0, BLOCKS, look_step, 0)
    bound = jnp.max(jnp.max(jnp.abs(table), axis=0, keepdims=True), axis=1, keepdims=True) + 6.0
    left_over = bound * 2.0**60
    scale = jnp.full_like(bound, 2.0**60)
    for step in (64, 32, 16, 8, 4, 2, 1):
        large = left_over >= 2.0**step
        left_over = jnp.where(large, left_over * 2.0**-step, left_over)
        scale = jnp.where(large, scale * 2.0**-step, scale)
    back = jnp.full_like(scale, 2.0**-7) / scale
    scale = scale * 2.0**7
    adjusted = (g_ref[...] + hess * row_mean_ref[...]).astype(BF).astype(F32)
    left_terms(0, adjusted * scale)
    left_rows((0, 1))

    low_half = lax.broadcasted_iota(I32, (8, 128), 1) < BINS

    def histogram(c):
        with jax.named_scope("mm"):
            hot = hot_ref[pl.ds(pl.multiple_of(512 * c, 512), 512), :]
            both = lax.dot_general(left_ref[...], hot, NT, preferred_element_type=F32)
            grad = (both[0:32] + both[32:64] * 0.0625) * back
            hess = (both[64:96] + both[96:128] * 0.0625) * (1.0 / 128.0)
            for to in range(NY):
                for pair in range(4):
                    a = grad[8 * to : 8 * to + 8, 128 * pair : 128 * pair + 128]
                    b = hess[8 * to : 8 * to + 8, 128 * pair : 128 * pair + 128]
                    out_y[c, to, 2 * pair] = jnp.where(low_half, a, pltpu.roll(b, 64, 1))
                    out_y[c, to, 2 * pair + 1] = jnp.where(low_half, pltpu.roll(a, 64, 1), b)

    def second_stage(c):
        with jax.named_scope("ywait"):
            wait_both(in_y.at[c], (y_send.at[c], y_recv.at[c]))
        for f in range(8):
            part = out_y[c, y, f] + in_y[c, 0, f] + in_y[c, 1, f] + in_y[c, 2, f]
            out_z[c, pl.ds(f, 8, stride=8), :] = part
        lines = pl.ds(pl.multiple_of(8 * c, 8), 8)
        for k in range(1, NZ):
            at = pl.ds(pl.multiple_of(8 * lax.rem(z + k, NZ), 8), 8)
            send(
                out_z.at[c, at], parts_ref.at[k - 1, lines], (z_send.at[c], z_recv.at[c]), z_peer(k)
            ).start()
        at = pl.ds(pl.multiple_of(8 * z, 8), 8)
        pltpu.make_async_copy(out_z.at[c, at], parts_ref.at[NZ - 1, lines], own_sem).start()

    def chunk(c, _):
        histogram(c)
        for k in range(1, NY):
            send(
                out_y.at[c, lax.rem(y + k, NY)], in_y.at[c, k - 1],
                (y_send.at[c], y_recv.at[c]), y_peer(k),
            ).start()

        @pl.when(c >= 2)
        def _():
            second_stage(c - 2)

        return 0

    lax.fori_loop(0, CHUNKS, chunk, 0)
    for c in (CHUNKS - 2, CHUNKS - 1):
        second_stage(c)
    with jax.named_scope("zwait"):
        for c in range(CHUNKS):
            wait_both(parts_ref.at[pl.ds(0, NZ - 1), pl.ds(8 * c, 8)], (z_send.at[c], z_recv.at[c]))
        wait(parts_ref.at[NZ - 1], own_sem)
    put_means.wait()


def last_sum(parts_ref, mean_ref, hist_ref, out_ref):
    total = parts_ref[0]
    for k in range(1, NZ):
        total = total + parts_ref[k]
    hist_ref[...] = total
    out_ref[...] = mean_ref[...]


def shards(gradient, hessian, groups, leaf_ids, bins, group_sizes, variance_ratio):
    count = gradient.shape[0]
    vmem, sem = pltpu.VMEM, pltpu.SemaphoreType.DMA
    whole = pl.BlockSpec(memory_space=pltpu.VMEM)
    parts, means = pl.pallas_call(
        kernel,
        out_shape=(jax.ShapeDtypeStruct((NZ, 32, 128), F32), jax.ShapeDtypeStruct((4, 128), F32)),
        in_specs=[whole] * 5
        + [pl.BlockSpec(memory_space=pltpu.SMEM), pl.BlockSpec(memory_space=pl.ANY)],
        out_specs=(pl.BlockSpec(memory_space=pl.ANY),) * 2,
        scratch_shapes=[
            vmem((32, count), I32),
            vmem((32 * BINS, count), F8),
            vmem((4 * LEAVES, count), F8),
            vmem((256, count), BF),
            vmem((5, 128, 128), I32),
            vmem((4, 128, 128), F32),
            vmem((128, 128), F32),
            vmem((16, 128), F32),
            vmem((NY - 1, 16, 128), F32),
            vmem((16, 128), F32),
            vmem((NZ - 1, 16, 128), F32),
            vmem((4, 128), F32),
            vmem((NY - 1, 4, 128), F32),
            vmem((16, 128), F32),
            vmem((16, 128), F32),
            vmem((128, 128), F32),
            vmem((CHUNKS, NY, 8, 8, 128), F32),
            vmem((CHUNKS, NY - 1, 8, 8, 128), F32),
            vmem((CHUNKS, 64, 128), F32),
            sem, sem, sem,
            sem((5,)), sem((5,)),
            sem((CHUNKS,)), sem((CHUNKS,)), sem((CHUNKS,)), sem((CHUNKS,)),
        ],
        compiler_params=pltpu.CompilerParams(
            collective_id=0, has_side_effects=True, vmem_limit_bytes=56 * 1024 * 1024
        ),
    )(
        gradient.reshape(128, 128),
        hessian.reshape(128, 128),
        groups.reshape(128, 128),
        leaf_ids.reshape(128, 128),
        group_sizes.reshape(4, 128),
        variance_ratio,
        bins,
    )
    hist, means = pl.pallas_call(
        last_sum,
        out_shape=(jax.ShapeDtypeStruct((32, 128), F32), jax.ShapeDtypeStruct((4, 128), F32)),
        in_specs=[whole] * 2,
        out_specs=(whole, whole),
    )(parts, means)
    return hist.reshape(1, 32, 128), means.reshape(512)


def solution(mesh):
    in_specs = (P("rows"), P("rows"), P("rows"), P("rows"), P("feat", "rows"), P("rows"), P())
    out_specs = (P("rows", "feat", None), P("rows"))
    return jax.shard_map(shards, mesh=mesh, in_specs=in_specs, out_specs=out_specs, check_vma=False)
```

```python
import functools

import jax
import jax.numpy as jnp
from jax import lax
from jax.experimental import pallas as pl
from jax.experimental.pallas import tpu as pltpu
from jax.sharding import PartitionSpec as P

BINS = 64
LEAVES = 32
F8 = jnp.float8_e4m3fn
BF = jnp.bfloat16
F32 = jnp.float32
I32 = jnp.int32
MESH = pl.DeviceIdType.MESH
NT = (((1,), (1,)), ((), ()))
NY, NZ, NF = 4, 8, 8
BLOCKS = 2
SUM_ROWS = 64
CHUNKS = 4
PARTS = (44, 64)
LOW_PART = 24
FAR_Y, FAR_Z, FAR_F = (2, 1, 3), (4, 3, 5, 2, 6, 1, 7), (4, 5, 3, 2, 6, 7, 1)


def iota0(dtype, rows, lanes):
    return lax.broadcasted_iota(I32, (rows, lanes), 0).astype(dtype)


def split(value, count):
    terms = []
    for _ in range(count):
        term = value.astype(BF).astype(F32)
        terms.append(term)
        value = value - term
    return terms


def kernel(
    g_hbm, h_hbm, group_hbm, leaf_hbm, size_hbm, ratio_ref, bins_hbm,
    parts_ref, mean_ref,
    g_ref, h_ref, group_ref, leaf_ref, size_ref, bins_ref, hot_ref, left_ref, low_hot_ref,
    ids_ref, term_ref, row_mean_ref,
    pay_ref, pay_in, mid_ref, mid_in, own_size_ref, size_in_y, size_z_ref, size_in_ref, table_ref,
    out_y, in_y, out_z,
    in_sem, mean_sem, own_sem, send_sem, recv_sem, y_send, y_recv, z_send, z_recv,
):
    rows, feat = lax.axis_index("rows"), lax.axis_index("feat")
    z, y = rows // NY, lax.rem(rows, NY)

    def y_peer(k):
        return (z * NY + lax.rem(y + k, NY), feat)

    def z_peer(k):
        return (lax.rem(z + k, NZ) * NY + y, feat)

    def f_peer(k):
        return (rows, lax.rem(feat + k, NF))

    def send(src, dst, sems, peer):
        return pltpu.make_async_remote_copy(
            src_ref=src, dst_ref=dst, send_sem=sems[0], recv_sem=sems[1],
            device_id=peer, device_id_type=MESH,
        )

    def wait(ref, sem):
        pltpu.make_async_copy(ref, ref, sem).wait()

    def wait_both(ref, sems):
        for sem in sems:
            wait(ref, sem)

    pay_sems, size_sems, mid_sems, far_sems, table_sems = [
        (send_sem.at[n], recv_sem.at[n]) for n in range(5)
    ]

    barrier = pltpu.get_barrier_semaphore()
    for peer in (
        [y_peer(k) for k in range(1, NY)]
        + [z_peer(k) for k in range(1, NZ)]
        + [f_peer(k) for k in range(1, NF)]
    ):
        pl.semaphore_signal(barrier, inc=1, device_id=peer, device_id_type=MESH)
    fetches = [
        pltpu.make_async_copy(src, dst, in_sem.at[n])
        for n, (src, dst) in enumerate(
            (
                (group_hbm, group_ref),
                (g_hbm, g_ref),
                (leaf_hbm, leaf_ref),
                (h_hbm, h_ref),
                (size_hbm, size_ref),
                (bins_hbm, bins_ref),
            )
        )
    ]
    for fetch in fetches:
        fetch.start()
    with jax.named_scope("fetch"):
        for fetch in fetches[:5]:
            fetch.wait()

    ids = group_ref[...]
    high, low = lax.shift_right_logical(ids, 7), ids & 127
    ids_ref[0] = high - 16 * feat
    ids_ref[1] = low
    ids_ref[2] = low + 2 * (high & 64)
    ids_ref[3] = high & 63
    leaf = leaf_ref[...]
    ids_ref[4] = (leaf & (NY - 1)) * NZ + lax.shift_right_logical(leaf, 2)
    for n, term in enumerate(split(g_ref[...], 3)):
        term_ref[n] = term

    def sum_step(n, total):
        left, right = [], []
        for t in range(SUM_ROWS):
            row = pl.ds(SUM_ROWS * n + t, 1)
            wide = jnp.broadcast_to(ids_ref[1, row, :], (128, 128)).astype(jnp.int16)
            right.append(jnp.where(wide == iota0(jnp.int16, 128, 128), BF(1), BF(0)))
            wide = jnp.broadcast_to(ids_ref[0, row, :], (16, 128)).astype(jnp.int16)
            own = wide == iota0(jnp.int16, 16, 128)
            values = [
                jnp.where(own, jnp.broadcast_to(term_ref[n, row, :], (16, 128)).astype(BF), BF(0))
                for n in range(3)
            ]
            left.append(jnp.concatenate(values, 0))
        return total + lax.dot_general(
            jnp.concatenate(left, 1), jnp.concatenate(right, 1), NT, preferred_element_type=F32
        )

    with jax.named_scope("gsum"):
        total = lax.fori_loop(0, 128 // SUM_ROWS, sum_step, jnp.zeros((48, 128), F32))
        pay_ref[...] = total[0:16] + total[16:32] + total[32:48]
    own_size_ref[...] = size_ref[...].astype(F32)

    with jax.named_scope("bar"):
        pl.semaphore_wait(barrier, NY + NZ + NF - 3)

    def hot_step(t, _):
        lanes = pl.ds(pl.multiple_of(256 * t, 256), 256)
        for f in range(32):
            wide = jnp.broadcast_to(bins_ref[f : f + 1, lanes], (BINS, 256)).astype(jnp.int8)
            hot_ref[BINS * f : BINS * (f + 1), lanes] = jnp.where(
                wide == iota0(jnp.int8, BINS, 256), F8(1), F8(0)
            )
        return 0

    def build(first, last):
        with jax.named_scope("build"):
            lax.fori_loop(first, last, hot_step, 0)

    def left_rows(parts):
        def step(t, _):
            for u in range(16):
                row = pl.ds(16 * t + u, 1)
                wide = jnp.broadcast_to(ids_ref[4, row, :], (LEAVES, 128)).astype(jnp.int8)
                member = wide == iota0(jnp.int8, LEAVES, 128)
                at = pl.ds(pl.multiple_of(2048 * t + 128 * u, 128), 128)
                for c in parts:
                    term = jnp.broadcast_to(term_ref[c, row, :], (LEAVES, 128)).astype(F8)
                    left_ref[LEAVES * c : LEAVES * (c + 1), at] = jnp.where(member, term, F8(0))
            return 0

        with jax.named_scope("left"):
            lax.fori_loop(0, 8, step, 0)

    def left_terms(c, value):
        first = value.astype(F8).astype(F32)
        term_ref[c] = first
        term_ref[c + 1] = ((value - first) * 16.0).astype(F8).astype(F32)

    for k in FAR_Y:
        send(pay_ref, pay_in.at[k - 1], pay_sems, y_peer(k)).start()
    for k in FAR_Y:
        send(own_size_ref, size_in_y.at[k - 1], size_sems, y_peer(k)).start()
    def low_hot_step(t, _):
        for u in range(4):
            wide = jnp.broadcast_to(ids_ref[2, pl.ds(4 * t + u, 1), :], (256, 128))
            at = pl.ds(pl.multiple_of(512 * t + 128 * u, 128), 128)
            low_hot_ref[:, at] = jnp.where(
                wide.astype(jnp.int16) == iota0(jnp.int16, 256, 128), BF(1), BF(0)
            )
        return 0

    with jax.named_scope("lowhot"):
        lax.fori_loop(0, LOW_PART, low_hot_step, 0)
    hess = h_ref[...].astype(F32)
    left_terms(2, hess * 128.0)
    left_rows((2, 3))
    with jax.named_scope("cwait"):
        wait_both(pay_in, pay_sems)
    mid_ref[...] = pay_ref[...] + pay_in[0] + pay_in[1] + pay_in[2]

    for k in FAR_Z:
        send(mid_ref, mid_in.at[k - 1], mid_sems, z_peer(k)).start()
    wait_both(size_in_y, size_sems)
    size_z_ref[pl.ds(pl.multiple_of(4 * y, 4), 4), :] = own_size_ref[...]
    for k in range(1, NY):
        at = pl.ds(pl.multiple_of(4 * lax.rem(y + NY - k, NY), 4), 4)
        size_z_ref[at, :] = size_in_y[k - 1]

    @pl.when(z == feat)
    def _():
        for k in FAR_Z:
            send(size_z_ref, size_in_ref, far_sems, z_peer(k)).start()

    fetches[5].wait()
    build(0, PARTS[0])

    with jax.named_scope("cwait"):
        wait_both(mid_in, mid_sems)

    @pl.when(z == feat)
    def _():
        wait(mid_in, far_sems[0])
        size_in_ref[...] = size_z_ref[...]

    @pl.when(z != feat)
    def _():
        wait(size_in_ref, far_sems[1])

    total = mid_ref[...]
    for k in range(NZ - 1):
        total = total + mid_in[k]
    mine = pl.ds(pl.multiple_of(16 * feat, 16), 16)
    table_ref[mine, :] = -total / (size_in_ref[...] + ratio_ref[0])

    for k in FAR_F:
        send(table_ref.at[mine], table_ref.at[mine], table_sems, f_peer(k)).start()
    with jax.named_scope("lowhot"):
        lax.fori_loop(LOW_PART, 32, low_hot_step, 0)
    build(PARTS[0], PARTS[1])
    with jax.named_scope("cwait"):
        wait_both(table_ref.at[pl.ds(0, 16 * (NF - 1))], table_sems)

    table = table_ref[...]
    put_means = pltpu.make_async_copy(
        table_ref.at[pl.ds(pl.multiple_of(4 * rows, 4), 4)], mean_ref, mean_sem
    )
    put_means.start()
    wide = jnp.concatenate([table[0:64], table[64:128]], 1)
    wide = jnp.concatenate(split(wide, 2), 0).astype(BF)
    def look_step(block, _):
        span = 16384 // BLOCKS
        lanes = pl.ds(pl.multiple_of(span * block, span), span)
        found = jnp.dot(wide, low_hot_ref[:, lanes], preferred_element_type=F32)
        for u in range(span // 128):
            row = pl.ds(block * (span // 128) + u, 1)
            at = slice(128 * u, 128 * u + 128)
            part = found[0:64, at] + found[64:128, at]
            own = jnp.broadcast_to(ids_ref[3, row, :], (64, 128)) == iota0(I32, 64, 128)
            row_mean_ref[row, :] = jnp.sum(jnp.where(own, part, 0.0), axis=0, keepdims=True)
        return 0

    with jax.named_scope("look"):
        lax.fori_loop(0, BLOCKS, look_step, 0)
    bound = jnp.max(jnp.max(jnp.abs(table), axis=0, keepdims=True), axis=1, keepdims=True) + 6.0
    left_over = bound * 2.0**60
    scale = jnp.full_like(bound, 2.0**60)
    for step in (64, 32, 16, 8, 4, 2, 1):
        large = left_over >= 2.0**step
        left_over = jnp.where(large, left_over * 2.0**-step, left_over)
        scale = jnp.where(large, scale * 2.0**-step, scale)
    back = jnp.full_like(scale, 2.0**-7) / scale
    scale = scale * 2.0**7
    adjusted = (g_ref[...] + hess * row_mean_ref[...]).astype(BF).astype(F32)
    left_terms(0, adjusted * scale)
    left_rows((0, 1))

    low_half = lax.broadcasted_iota(I32, (8, 128), 1) < BINS

    def histogram(c):
        with jax.named_scope("mm"):
            hot = hot_ref[pl.ds(pl.multiple_of(512 * c, 512), 512), :]
            both = lax.dot_general(left_ref[...], hot, NT, preferred_element_type=F32)
            grad = (both[0:32] + both[32:64] * 0.0625) * back
            hess = (both[64:96] + both[96:128] * 0.0625) * (1.0 / 128.0)
            for to in range(NY):
                for pair in range(4):
                    a = grad[8 * to : 8 * to + 8, 128 * pair : 128 * pair + 128]
                    b = hess[8 * to : 8 * to + 8, 128 * pair : 128 * pair + 128]
                    out_y[c, to, 2 * pair] = jnp.where(low_half, a, pltpu.roll(b, 64, 1))
                    out_y[c, to, 2 * pair + 1] = jnp.where(low_half, pltpu.roll(a, 64, 1), b)

    def second_stage(c):
        with jax.named_scope("ywait"):
            wait_both(in_y.at[c], (y_send.at[c], y_recv.at[c]))
        for f in range(8):
            part = out_y[c, y, f] + in_y[c, 0, f] + in_y[c, 1, f] + in_y[c, 2, f]
            out_z[c, pl.ds(f, 8, stride=8), :] = part
        lines = pl.ds(pl.multiple_of(8 * c, 8), 8)
        for k in FAR_Z:
            at = pl.ds(pl.multiple_of(8 * lax.rem(z + k, NZ), 8), 8)
            send(
                out_z.at[c, at], parts_ref.at[k - 1, lines], (z_send.at[c], z_recv.at[c]), z_peer(k)
            ).start()
        at = pl.ds(pl.multiple_of(8 * z, 8), 8)
        pltpu.make_async_copy(out_z.at[c, at], parts_ref.at[NZ - 1, lines], own_sem).start()

    def chunk(c, _):
        histogram(c)
        for k in FAR_Y:
            send(
                out_y.at[c, lax.rem(y + k, NY)], in_y.at[c, k - 1],
                (y_send.at[c], y_recv.at[c]), y_peer(k),
            ).start()

        @pl.when(c >= 2)
        def _():
            second_stage(c - 2)

        return 0

    lax.fori_loop(0, CHUNKS, chunk, 0)
    for c in (CHUNKS - 2, CHUNKS - 1):
        second_stage(c)
    with jax.named_scope("zwait"):
        for c in range(CHUNKS):
            wait_both(parts_ref.at[pl.ds(0, NZ - 1), pl.ds(8 * c, 8)], (z_send.at[c], z_recv.at[c]))
        wait(parts_ref.at[NZ - 1], own_sem)
    put_means.wait()


def last_sum(parts_ref, mean_ref, hist_ref, out_ref):
    total = parts_ref[0]
    for k in range(1, NZ):
        total = total + parts_ref[k]
    hist_ref[...] = total
    out_ref[...] = mean_ref[...]


def shards(gradient, hessian, groups, leaf_ids, bins, group_sizes, variance_ratio):
    count = gradient.shape[0]
    vmem, sem = pltpu.VMEM, pltpu.SemaphoreType.DMA
    whole = pl.BlockSpec(memory_space=pltpu.VMEM)
    parts, means = pl.pallas_call(
        kernel,
        out_shape=(jax.ShapeDtypeStruct((NZ, 32, 128), F32), jax.ShapeDtypeStruct((4, 128), F32)),
        in_specs=[pl.BlockSpec(memory_space=pl.ANY)] * 5
        + [pl.BlockSpec(memory_space=pltpu.SMEM), pl.BlockSpec(memory_space=pl.ANY)],
        out_specs=(pl.BlockSpec(memory_space=pl.ANY),) * 2,
        scratch_shapes=[
            vmem((128, 128), F32),
            vmem((128, 128), BF),
            vmem((128, 128), I32),
            vmem((128, 128), I32),
            vmem((4, 128), I32),
            vmem((32, count), I32),
            vmem((32 * BINS, count), F8),
            vmem((4 * LEAVES, count), F8),
            vmem((256, count), BF),
            vmem((5, 128, 128), I32),
            vmem((4, 128, 128), F32),
            vmem((128, 128), F32),
            vmem((16, 128), F32),
            vmem((NY - 1, 16, 128), F32),
            vmem((16, 128), F32),
            vmem((NZ - 1, 16, 128), F32),
            vmem((4, 128), F32),
            vmem((NY - 1, 4, 128), F32),
            vmem((16, 128), F32),
            vmem((16, 128), F32),
            vmem((128, 128), F32),
            vmem((CHUNKS, NY, 8, 8, 128), F32),
            vmem((CHUNKS, NY - 1, 8, 8, 128), F32),
            vmem((CHUNKS, 64, 128), F32),
            sem((6,)), sem, sem,
            sem((5,)), sem((5,)),
            sem((CHUNKS,)), sem((CHUNKS,)), sem((CHUNKS,)), sem((CHUNKS,)),
        ],
        compiler_params=pltpu.CompilerParams(
            collective_id=0, has_side_effects=True, vmem_limit_bytes=56 * 1024 * 1024
        ),
    )(
        gradient.reshape(128, 128),
        hessian.reshape(128, 128),
        groups.reshape(128, 128),
        leaf_ids.reshape(128, 128),
        group_sizes.reshape(4, 128),
        variance_ratio,
        bins,
    )
    hist, means = pl.pallas_call(
        last_sum,
        out_shape=(jax.ShapeDtypeStruct((32, 128), F32), jax.ShapeDtypeStruct((4, 128), F32)),
        in_specs=[whole] * 2,
        out_specs=(whole, whole),
    )(parts, means)
    return hist.reshape(1, 32, 128), means.reshape(512)


def solution(mesh):
    in_specs = (P("rows"), P("rows"), P("rows"), P("rows"), P("feat", "rows"), P("rows"), P())
    out_specs = (P("rows", "feat", None), P("rows"))
    return jax.shard_map(shards, mesh=mesh, in_specs=in_specs, out_specs=out_specs, check_vma=False)
```

```python
import functools

import jax
import jax.numpy as jnp
from jax import lax
from jax.experimental import pallas as pl
from jax.experimental.pallas import tpu as pltpu
from jax.sharding import PartitionSpec as P

BINS = 64
LEAVES = 32
F8 = jnp.float8_e4m3fn
BF = jnp.bfloat16
F32 = jnp.float32
I32 = jnp.int32
MESH = pl.DeviceIdType.MESH
NT = (((1,), (1,)), ((), ()))
NY, NZ, NF = 4, 8, 8
BLOCKS = 2
SUM_ROWS = 64
CHUNKS = 4
LOW_FIRST, BUILD_FIRST = (32, 16), (54, 44)
FAR_Y, FAR_Z = (2, 1, 3), (4, 3, 5, 2, 6, 1, 7)
FAR_F = ((2, 0), (1, 0), (3, 0), (2, 1), (1, 1), (3, 1), (0, 0))


def iota0(dtype, rows, lanes):
    return lax.broadcasted_iota(I32, (rows, lanes), 0).astype(dtype)


def split(value, count):
    terms = []
    for _ in range(count):
        term = value.astype(BF).astype(F32)
        terms.append(term)
        value = value - term
    return terms


def kernel(
    g_hbm, h_hbm, group_hbm, leaf_hbm, size_hbm, ratio_ref, bins_hbm,
    parts_ref, mean_ref,
    g_ref, h_ref, group_ref, leaf_ref, size_ref, bins_ref, hot_ref, left_ref, low_hot_ref,
    ids_ref, term_ref, row_mean_ref,
    pay_ref, pay_in, mid_ref, mid_in, own_size_ref, size_in_y, size_z_ref, size_in_ref, table_ref,
    out_y, in_y, out_z,
    in_sem, mean_sem, own_sem, send_sem, recv_sem, y_send, y_recv, z_send, z_recv,
):
    rows, feat = lax.axis_index("rows"), lax.axis_index("feat")
    z, y = rows // NY, lax.rem(rows, NY)
    x, core = feat // 2, lax.rem(feat, 2)

    def y_peer(k):
        return (z * NY + lax.rem(y + k, NY), feat)

    def z_peer(k):
        return (lax.rem(z + k, NZ) * NY + y, feat)

    def f_peer(k):
        return (rows, lax.rem(feat + k, NF))

    def send(src, dst, sems, peer):
        return pltpu.make_async_remote_copy(
            src_ref=src, dst_ref=dst, send_sem=sems[0], recv_sem=sems[1],
            device_id=peer, device_id_type=MESH,
        )

    def wait(ref, sem):
        pltpu.make_async_copy(ref, ref, sem).wait()

    def wait_both(ref, sems):
        for sem in sems:
            wait(ref, sem)

    pay_sems, size_sems, mid_sems, far_sems, table_sems = [
        (send_sem.at[n], recv_sem.at[n]) for n in range(5)
    ]

    barrier = pltpu.get_barrier_semaphore()
    for peer in (
        [y_peer(k) for k in range(1, NY)]
        + [z_peer(k) for k in range(1, NZ)]
        + [f_peer(k) for k in range(1, NF)]
    ):
        pl.semaphore_signal(barrier, inc=1, device_id=peer, device_id_type=MESH)
    fetches = [
        pltpu.make_async_copy(src, dst, in_sem.at[n])
        for n, (src, dst) in enumerate(
            (
                (group_hbm, group_ref),
                (g_hbm, g_ref),
                (leaf_hbm, leaf_ref),
                (h_hbm, h_ref),
                (size_hbm, size_ref),
                (bins_hbm, bins_ref),
            )
        )
    ]
    for fetch in fetches:
        fetch.start()
    with jax.named_scope("fetch"):
        for fetch in fetches[:5]:
            fetch.wait()

    ids = group_ref[...]
    high, low = lax.shift_right_logical(ids, 7), ids & 127
    ids_ref[0] = high - 32 * x
    ids_ref[1] = low
    ids_ref[2] = low + 2 * (high & 64)
    ids_ref[3] = high & 63
    leaf = leaf_ref[...]
    ids_ref[4] = (leaf & (NY - 1)) * NZ + lax.shift_right_logical(leaf, 2)
    for n, term in enumerate(split(g_ref[...], 3)):
        term_ref[n] = term

    def sum_step(n, total):
        left, right = [], []
        for t in range(SUM_ROWS):
            row = pl.ds(SUM_ROWS * n + t, 1)
            wide = jnp.broadcast_to(ids_ref[1, row, :], (128, 128)).astype(jnp.int16)
            right.append(jnp.where(wide == iota0(jnp.int16, 128, 128), BF(1), BF(0)))
            wide = jnp.broadcast_to(ids_ref[0, row, :], (32, 128)).astype(jnp.int16)
            own = wide == iota0(jnp.int16, 32, 128)
            values = [
                jnp.where(own, jnp.broadcast_to(term_ref[n, row, :], (32, 128)).astype(BF), BF(0))
                for n in range(3)
            ]
            left.append(jnp.concatenate(values, 0))
        return total + lax.dot_general(
            jnp.concatenate(left, 1), jnp.concatenate(right, 1), NT, preferred_element_type=F32
        )

    @pl.when(core == 1)
    def _():
        with jax.named_scope("gsum"):
            total = lax.fori_loop(0, 128 // SUM_ROWS, sum_step, jnp.zeros((96, 128), F32))
            pay_ref[...] = total[0:32] + total[32:64] + total[64:96]

    own_size_ref[...] = size_ref[...].astype(F32)

    with jax.named_scope("bar"):
        pl.semaphore_wait(barrier, NY + NZ + NF - 3)

    def hot_step(t, _):
        lanes = pl.ds(pl.multiple_of(256 * t, 256), 256)
        for f in range(32):
            wide = jnp.broadcast_to(bins_ref[f : f + 1, lanes], (BINS, 256)).astype(jnp.int8)
            hot_ref[BINS * f : BINS * (f + 1), lanes] = jnp.where(
                wide == iota0(jnp.int8, BINS, 256), F8(1), F8(0)
            )
        return 0

    def build(first, last):
        with jax.named_scope("build"):
            lax.fori_loop(first, last, hot_step, 0)

    def left_rows(parts):
        def step(t, _):
            for u in range(16):
                row = pl.ds(16 * t + u, 1)
                wide = jnp.broadcast_to(ids_ref[4, row, :], (LEAVES, 128)).astype(jnp.int8)
                member = wide == iota0(jnp.int8, LEAVES, 128)
                at = pl.ds(pl.multiple_of(2048 * t + 128 * u, 128), 128)
                for c in parts:
                    term = jnp.broadcast_to(term_ref[c, row, :], (LEAVES, 128)).astype(F8)
                    left_ref[LEAVES * c : LEAVES * (c + 1), at] = jnp.where(member, term, F8(0))
            return 0

        with jax.named_scope("left"):
            lax.fori_loop(0, 8, step, 0)

    def left_terms(c, value):
        first = value.astype(F8).astype(F32)
        term_ref[c] = first
        term_ref[c + 1] = ((value - first) * 16.0).astype(F8).astype(F32)

    @pl.when(core == 1)
    def _():
        for k in FAR_Y:
            send(pay_ref, pay_in.at[k - 1], pay_sems, y_peer(k)).start()
        for k in FAR_Y:
            send(own_size_ref, size_in_y.at[k - 1], size_sems, y_peer(k)).start()

    low_first = jnp.where(core == 1, LOW_FIRST[1], LOW_FIRST[0])
    build_first = jnp.where(core == 1, BUILD_FIRST[1], BUILD_FIRST[0])

    def low_hot_step(t, _):
        for u in range(4):
            wide = jnp.broadcast_to(ids_ref[2, pl.ds(4 * t + u, 1), :], (256, 128))
            at = pl.ds(pl.multiple_of(512 * t + 128 * u, 128), 128)
            low_hot_ref[:, at] = jnp.where(
                wide.astype(jnp.int16) == iota0(jnp.int16, 256, 128), BF(1), BF(0)
            )
        return 0

    with jax.named_scope("lowhot"):
        lax.fori_loop(0, low_first, low_hot_step, 0)
    hess = h_ref[...].astype(F32)
    left_terms(2, hess * 128.0)
    left_rows((2, 3))
    @pl.when(core == 1)
    def _():
        with jax.named_scope("cwait"):
            wait_both(pay_in, pay_sems)
        mid_ref[...] = pay_ref[...] + pay_in[0] + pay_in[1] + pay_in[2]
        for k in FAR_Z:
            send(mid_ref, mid_in.at[k - 1], mid_sems, z_peer(k)).start()
        wait_both(size_in_y, size_sems)
        size_z_ref[pl.ds(pl.multiple_of(4 * y, 4), 4), :] = own_size_ref[...]
        for k in range(1, NY):
            at = pl.ds(pl.multiple_of(4 * lax.rem(y + NY - k, NY), 4), 4)
            size_z_ref[at, :] = size_in_y[k - 1]

    has_sizes = (core == 1) & (z // 2 == x)
    size_rows = pl.ds(pl.multiple_of(16 * lax.rem(z, 2), 16), 16)

    @pl.when(has_sizes)
    def _():
        for k in FAR_Z:
            send(size_z_ref, size_in_ref.at[size_rows], far_sems, z_peer(k)).start()

    fetches[5].wait()
    build(0, build_first)

    @pl.when(core == 1)
    def _():
        with jax.named_scope("cwait"):
            wait_both(mid_in, mid_sems)

    @pl.when(has_sizes)
    def _():
        wait(mid_in.at[:, pl.ds(0, 16)], far_sems[0])
        wait(size_z_ref, far_sems[1])
        size_in_ref[size_rows, :] = size_z_ref[...]

    @pl.when((core == 1) & (z // 2 != x))
    def _():
        wait(size_in_ref, far_sems[1])

    mine = pl.ds(pl.multiple_of(32 * x, 32), 32)

    @pl.when(core == 1)
    def _():
        total = mid_ref[...]
        for k in range(NZ - 1):
            total = total + mid_in[k]
        table_ref[mine, :] = -total / (size_in_ref[...] + ratio_ref[0])
        for k, to in FAR_F:
            peer = (rows, 2 * lax.rem(x + k, 4) + to)
            send(table_ref.at[mine], table_ref.at[mine], table_sems, peer).start()

    with jax.named_scope("lowhot"):
        lax.fori_loop(low_first, 32, low_hot_step, 0)
    build(build_first, 64)

    with jax.named_scope("cwait"):

        @pl.when(core == 1)
        def _():
            wait(mid_in, table_sems[0])
            wait(table_ref.at[pl.ds(0, 96)], table_sems[1])

        @pl.when(core == 0)
        def _():
            wait(table_ref, table_sems[1])

    table = table_ref[...]
    put_means = pltpu.make_async_copy(
        table_ref.at[pl.ds(pl.multiple_of(4 * rows, 4), 4)], mean_ref, mean_sem
    )
    put_means.start()
    wide = jnp.concatenate([table[0:64], table[64:128]], 1)
    wide = jnp.concatenate(split(wide, 2), 0).astype(BF)
    def look_step(block, _):
        span = 16384 // BLOCKS
        lanes = pl.ds(pl.multiple_of(span * block, span), span)
        found = jnp.dot(wide, low_hot_ref[:, lanes], preferred_element_type=F32)
        for u in range(span // 128):
            row = pl.ds(block * (span // 128) + u, 1)
            at = slice(128 * u, 128 * u + 128)
            part = found[0:64, at] + found[64:128, at]
            own = jnp.broadcast_to(ids_ref[3, row, :], (64, 128)) == iota0(I32, 64, 128)
            row_mean_ref[row, :] = jnp.sum(jnp.where(own, part, 0.0), axis=0, keepdims=True)
        return 0

    with jax.named_scope("look"):
        lax.fori_loop(0, BLOCKS, look_step, 0)
    bound = jnp.max(jnp.max(jnp.abs(table), axis=0, keepdims=True), axis=1, keepdims=True) + 6.0
    left_over = bound * 2.0**60
    scale = jnp.full_like(bound, 2.0**60)
    for step in (64, 32, 16, 8, 4, 2, 1):
        large = left_over >= 2.0**step
        left_over = jnp.where(large, left_over * 2.0**-step, left_over)
        scale = jnp.where(large, scale * 2.0**-step, scale)
    back = jnp.full_like(scale, 2.0**-7) / scale
    scale = scale * 2.0**7
    adjusted = (g_ref[...] + hess * row_mean_ref[...]).astype(BF).astype(F32)
    left_terms(0, adjusted * scale)
    left_rows((0, 1))

    low_half = lax.broadcasted_iota(I32, (8, 128), 1) < BINS

    def histogram(c, first, count):
        with jax.named_scope("mm"):
            start = pl.multiple_of(512 * c + BINS * first, BINS * count)
            hot = hot_ref[pl.ds(start, BINS * count), :]
            both = lax.dot_general(left_ref[...], hot, NT, preferred_element_type=F32)
            grad = (both[0:32] + both[32:64] * 0.0625) * back
            hess = (both[64:96] + both[96:128] * 0.0625) * (1.0 / 128.0)
            for to in range(NY):
                for pair in range(count // 2):
                    a = grad[8 * to : 8 * to + 8, 128 * pair : 128 * pair + 128]
                    b = hess[8 * to : 8 * to + 8, 128 * pair : 128 * pair + 128]
                    f = first + 2 * pair
                    out_y[c, to, f] = jnp.where(low_half, a, pltpu.roll(b, 64, 1))
                    out_y[c, to, f + 1] = jnp.where(low_half, pltpu.roll(a, 64, 1), b)
        at = pl.ds(first, count)
        for k in FAR_Y:
            send(
                out_y.at[c, lax.rem(y + k, NY), at], in_y.at[c, k - 1, at],
                (y_send.at[c], y_recv.at[c]), y_peer(k),
            ).start()

    def second_stage(c):
        with jax.named_scope("ywait"):
            wait_both(in_y.at[c], (y_send.at[c], y_recv.at[c]))
        for f in range(8):
            part = out_y[c, y, f] + in_y[c, 0, f] + in_y[c, 1, f] + in_y[c, 2, f]
            out_z[c, pl.ds(f, 8, stride=8), :] = part
        lines = pl.ds(pl.multiple_of(8 * c, 8), 8)
        for k in FAR_Z:
            at = pl.ds(pl.multiple_of(8 * lax.rem(z + k, NZ), 8), 8)
            send(
                out_z.at[c, at], parts_ref.at[k - 1, lines], (z_send.at[c], z_recv.at[c]), z_peer(k)
            ).start()
        at = pl.ds(pl.multiple_of(8 * z, 8), 8)
        pltpu.make_async_copy(out_z.at[c, at], parts_ref.at[NZ - 1, lines], own_sem).start()

    def chunk(c, _):
        histogram(c, 0, 8)

        @pl.when(c >= 2)
        def _():
            second_stage(c - 2)

        return 0

    def last_chunk(n, _):
        histogram(CHUNKS - 1, 4 * n, 4)
        second_stage(CHUNKS - 3 + n)
        return 0

    lax.fori_loop(0, CHUNKS - 1, chunk, 0)
    lax.fori_loop(0, 2, last_chunk, 0)
    second_stage(CHUNKS - 1)
    with jax.named_scope("zwait"):
        for c in range(CHUNKS):
            wait_both(parts_ref.at[pl.ds(0, NZ - 1), pl.ds(8 * c, 8)], (z_send.at[c], z_recv.at[c]))
        wait(parts_ref.at[NZ - 1], own_sem)
    put_means.wait()


def last_sum(parts_ref, mean_ref, hist_ref, out_ref):
    total = parts_ref[0]
    for k in range(1, NZ):
        total = total + parts_ref[k]
    hist_ref[...] = total
    out_ref[...] = mean_ref[...]


def shards(gradient, hessian, groups, leaf_ids, bins, group_sizes, variance_ratio):
    count = gradient.shape[0]
    vmem, sem = pltpu.VMEM, pltpu.SemaphoreType.DMA
    whole = pl.BlockSpec(memory_space=pltpu.VMEM)
    parts, means = pl.pallas_call(
        kernel,
        out_shape=(jax.ShapeDtypeStruct((NZ, 32, 128), F32), jax.ShapeDtypeStruct((4, 128), F32)),
        in_specs=[pl.BlockSpec(memory_space=pl.ANY)] * 5
        + [pl.BlockSpec(memory_space=pltpu.SMEM), pl.BlockSpec(memory_space=pl.ANY)],
        out_specs=(pl.BlockSpec(memory_space=pl.ANY),) * 2,
        scratch_shapes=[
            vmem((128, 128), F32),
            vmem((128, 128), BF),
            vmem((128, 128), I32),
            vmem((128, 128), I32),
            vmem((4, 128), I32),
            vmem((32, count), I32),
            vmem((32 * BINS, count), F8),
            vmem((4 * LEAVES, count), F8),
            vmem((256, count), BF),
            vmem((5, 128, 128), I32),
            vmem((4, 128, 128), F32),
            vmem((128, 128), F32),
            vmem((32, 128), F32),
            vmem((NY - 1, 32, 128), F32),
            vmem((32, 128), F32),
            vmem((NZ - 1, 32, 128), F32),
            vmem((4, 128), F32),
            vmem((NY - 1, 4, 128), F32),
            vmem((16, 128), F32),
            vmem((32, 128), F32),
            vmem((128, 128), F32),
            vmem((CHUNKS, NY, 8, 8, 128), F32),
            vmem((CHUNKS, NY - 1, 8, 8, 128), F32),
            vmem((CHUNKS, 64, 128), F32),
            sem((6,)), sem, sem,
            sem((5,)), sem((5,)),
            sem((CHUNKS,)), sem((CHUNKS,)), sem((CHUNKS,)), sem((CHUNKS,)),
        ],
        compiler_params=pltpu.CompilerParams(
            collective_id=0, has_side_effects=True, vmem_limit_bytes=56 * 1024 * 1024
        ),
    )(
        gradient.reshape(128, 128),
        hessian.reshape(128, 128),
        groups.reshape(128, 128),
        leaf_ids.reshape(128, 128),
        group_sizes.reshape(4, 128),
        variance_ratio,
        bins,
    )
    hist, means = pl.pallas_call(
        last_sum,
        out_shape=(jax.ShapeDtypeStruct((32, 128), F32), jax.ShapeDtypeStruct((4, 128), F32)),
        in_specs=[whole] * 2,
        out_specs=(whole, whole),
    )(parts, means)
    return hist.reshape(1, 32, 128), means.reshape(512)


def solution(mesh):
    in_specs = (P("rows"), P("rows"), P("rows"), P("rows"), P("feat", "rows"), P("rows"), P())
    out_specs = (P("rows", "feat", None), P("rows"))
    return jax.shard_map(shards, mesh=mesh, in_specs=in_specs, out_specs=out_specs, check_vma=False)
```

```python
import functools

import jax
import jax.numpy as jnp
from jax import lax
from jax.experimental import pallas as pl
from jax.experimental.pallas import tpu as pltpu
from jax.sharding import PartitionSpec as P

BINS = 64
LEAVES = 32
F8 = jnp.float8_e4m3fn
BF = jnp.bfloat16
F32 = jnp.float32
I32 = jnp.int32
MESH = pl.DeviceIdType.MESH
NT = (((1,), (1,)), ((), ()))
NY, NZ = 4, 8
BLOCKS = 2
SUM_ROWS = 64
CHUNKS = 4
LOW_FIRST, BUILD_FIRST = (32, 16), (54, 44)
FAR_Y, FAR_Z = (2, 1, 3), (4, 3, 5, 2, 6, 1, 7)
FAR_F = ((2, 0), (1, 0), (3, 0), (2, 1), (1, 1), (3, 1), (0, 0))


def iota0(dtype, rows, lanes):
    return lax.broadcasted_iota(I32, (rows, lanes), 0).astype(dtype)


def split(value, count):
    terms = []
    for _ in range(count):
        term = value.astype(BF).astype(F32)
        terms.append(term)
        value = value - term
    return terms


def kernel(
    g_hbm, h_hbm, group_hbm, leaf_hbm, size_hbm, ratio_ref, bins_hbm,
    parts_ref, mean_ref,
    g_ref, h_ref, group_ref, leaf_ref, size_ref, bins_ref, hot_ref, left_ref, low_hot_ref,
    ids_ref, term_ref, row_mean_ref,
    pay_ref, pay_in, mid_ref, mid_in, own_size_ref, size_in_y, size_z_ref, size_in_ref, table_ref,
    out_y, in_y, out_z,
    in_sem, mean_sem, own_sem, send_sem, recv_sem, y_send, y_recv, z_send, z_recv,
):
    rows, feat = lax.axis_index("rows"), lax.axis_index("feat")
    z, y = rows // NY, lax.rem(rows, NY)
    x, core = feat // 2, lax.rem(feat, 2)

    def y_peer(k):
        return (z * NY + lax.rem(y + k, NY), feat)

    def z_peer(k):
        return (lax.rem(z + k, NZ) * NY + y, feat)

    def send(src, dst, sems, peer):
        return pltpu.make_async_remote_copy(
            src_ref=src, dst_ref=dst, send_sem=sems[0], recv_sem=sems[1],
            device_id=peer, device_id_type=MESH,
        )

    def wait(ref, sem):
        pltpu.make_async_copy(ref, ref, sem).wait()

    def wait_both(ref, sems):
        for sem in sems:
            wait(ref, sem)

    pay_sems, size_sems, mid_sems, far_sems, table_sems = [
        (send_sem.at[n], recv_sem.at[n]) for n in range(5)
    ]

    barrier = pltpu.get_barrier_semaphore()

    def tell(*peers):
        for peer in peers:
            pl.semaphore_signal(barrier, inc=1, device_id=peer, device_id_type=MESH)

    tell(*[z_peer(k) for k in FAR_Z], *[y_peer(k) for k in FAR_Y])
    tell(*[(rows, 2 * lax.rem(x + k, 4) + 1) for k in (2, 1, 3)])

    @pl.when(core == 0)
    def _():
        tell((rows, feat + 1))

    fetches = [
        pltpu.make_async_copy(src, dst, in_sem.at[n])
        for n, (src, dst) in enumerate(
            (
                (group_hbm, group_ref),
                (g_hbm, g_ref),
                (leaf_hbm, leaf_ref),
                (h_hbm, h_ref),
                (size_hbm, size_ref),
                (bins_hbm, bins_ref),
            )
        )
    ]
    for fetch in fetches:
        fetch.start()
    with jax.named_scope("fetch"):
        for fetch in fetches[:5]:
            fetch.wait()

    ids = group_ref[...]
    high, low = lax.shift_right_logical(ids, 7), ids & 127
    ids_ref[0] = high - 32 * x
    ids_ref[1] = low
    ids_ref[2] = low + 2 * (high & 64)
    ids_ref[3] = high & 63
    leaf = leaf_ref[...]
    ids_ref[4] = (leaf & (NY - 1)) * NZ + lax.shift_right_logical(leaf, 2)
    for n, term in enumerate(split(g_ref[...], 3)):
        term_ref[n] = term

    def sum_step(n, total):
        left, right = [], []
        for t in range(SUM_ROWS):
            row = pl.ds(SUM_ROWS * n + t, 1)
            wide = jnp.broadcast_to(ids_ref[1, row, :], (128, 128)).astype(jnp.int16)
            right.append(jnp.where(wide == iota0(jnp.int16, 128, 128), BF(1), BF(0)))
            wide = jnp.broadcast_to(ids_ref[0, row, :], (32, 128)).astype(jnp.int16)
            own = wide == iota0(jnp.int16, 32, 128)
            values = [
                jnp.where(own, jnp.broadcast_to(term_ref[n, row, :], (32, 128)).astype(BF), BF(0))
                for n in range(3)
            ]
            left.append(jnp.concatenate(values, 0))
        return total + lax.dot_general(
            jnp.concatenate(left, 1), jnp.concatenate(right, 1), NT, preferred_element_type=F32
        )

    @pl.when(core == 1)
    def _():
        with jax.named_scope("gsum"):
            total = lax.fori_loop(0, 128 // SUM_ROWS, sum_step, jnp.zeros((96, 128), F32))
            pay_ref[...] = total[0:32] + total[32:64] + total[64:96]

    own_size_ref[...] = size_ref[...].astype(F32)

    with jax.named_scope("bar"):
        pl.semaphore_wait(barrier, 10 + 7 * core)

    def hot_step(t, _):
        lanes = pl.ds(pl.multiple_of(256 * t, 256), 256)
        for f in range(32):
            wide = jnp.broadcast_to(bins_ref[f : f + 1, lanes], (BINS, 256)).astype(jnp.int8)
            hot_ref[BINS * f : BINS * (f + 1), lanes] = jnp.where(
                wide == iota0(jnp.int8, BINS, 256), F8(1), F8(0)
            )
        return 0

    def build(first, last):
        with jax.named_scope("build"):
            lax.fori_loop(first, last, hot_step, 0)

    def left_rows(parts):
        def step(t, _):
            for u in range(16):
                row = pl.ds(16 * t + u, 1)
                wide = jnp.broadcast_to(ids_ref[4, row, :], (LEAVES, 128)).astype(jnp.int8)
                member = wide == iota0(jnp.int8, LEAVES, 128)
                at = pl.ds(pl.multiple_of(2048 * t + 128 * u, 128), 128)
                for c in parts:
                    term = jnp.broadcast_to(term_ref[c, row, :], (LEAVES, 128)).astype(F8)
                    left_ref[LEAVES * c : LEAVES * (c + 1), at] = jnp.where(member, term, F8(0))
            return 0

        with jax.named_scope("left"):
            lax.fori_loop(0, 8, step, 0)

    def left_terms(c, value):
        first = value.astype(F8).astype(F32)
        term_ref[c] = first
        term_ref[c + 1] = ((value - first) * 16.0).astype(F8).astype(F32)

    @pl.when(core == 1)
    def _():
        for k in FAR_Y:
            send(pay_ref, pay_in.at[k - 1], pay_sems, y_peer(k)).start()
        for k in FAR_Y:
            send(own_size_ref, size_in_y.at[k - 1], size_sems, y_peer(k)).start()

    low_first = jnp.where(core == 1, LOW_FIRST[1], LOW_FIRST[0])
    build_first = jnp.where(core == 1, BUILD_FIRST[1], BUILD_FIRST[0])

    def low_hot_step(t, _):
        for u in range(4):
            wide = jnp.broadcast_to(ids_ref[2, pl.ds(4 * t + u, 1), :], (256, 128))
            at = pl.ds(pl.multiple_of(512 * t + 128 * u, 128), 128)
            low_hot_ref[:, at] = jnp.where(
                wide.astype(jnp.int16) == iota0(jnp.int16, 256, 128), BF(1), BF(0)
            )
        return 0

    with jax.named_scope("lowhot"):
        lax.fori_loop(0, low_first, low_hot_step, 0)
    hess = h_ref[...].astype(F32)
    left_terms(2, hess * 128.0)
    left_rows((2, 3))
    @pl.when(core == 1)
    def _():
        with jax.named_scope("cwait"):
            wait_both(pay_in, pay_sems)
        mid_ref[...] = pay_ref[...] + pay_in[0] + pay_in[1] + pay_in[2]
        for k in FAR_Z:
            send(mid_ref, mid_in.at[k - 1], mid_sems, z_peer(k)).start()
        wait_both(size_in_y, size_sems)
        size_z_ref[pl.ds(pl.multiple_of(4 * y, 4), 4), :] = own_size_ref[...]
        for k in range(1, NY):
            at = pl.ds(pl.multiple_of(4 * lax.rem(y + NY - k, NY), 4), 4)
            size_z_ref[at, :] = size_in_y[k - 1]

    has_sizes = (core == 1) & (z // 2 == x)
    size_rows = pl.ds(pl.multiple_of(16 * lax.rem(z, 2), 16), 16)

    @pl.when(has_sizes)
    def _():
        for k in FAR_Z:
            send(size_z_ref, size_in_ref.at[size_rows], far_sems, z_peer(k)).start()

    fetches[5].wait()
    build(0, build_first)

    @pl.when(core == 1)
    def _():
        with jax.named_scope("cwait"):
            wait_both(mid_in, mid_sems)

    @pl.when(has_sizes)
    def _():
        wait(mid_in.at[:, pl.ds(0, 16)], far_sems[0])
        wait(size_z_ref, far_sems[1])
        size_in_ref[size_rows, :] = size_z_ref[...]

    @pl.when((core == 1) & (z // 2 != x))
    def _():
        wait(size_in_ref, far_sems[1])

    mine = pl.ds(pl.multiple_of(32 * x, 32), 32)

    @pl.when(core == 1)
    def _():
        total = mid_ref[...]
        for k in range(NZ - 1):
            total = total + mid_in[k]
        table_ref[mine, :] = -total / (size_in_ref[...] + ratio_ref[0])
        for k, to in FAR_F:
            peer = (rows, 2 * lax.rem(x + k, 4) + to)
            send(table_ref.at[mine], table_ref.at[mine], table_sems, peer).start()

    with jax.named_scope("lowhot"):
        lax.fori_loop(low_first, 32, low_hot_step, 0)
    build(build_first, 64)

    with jax.named_scope("cwait"):

        @pl.when(core == 1)
        def _():
            wait(mid_in, table_sems[0])
            wait(table_ref.at[pl.ds(0, 96)], table_sems[1])

        @pl.when(core == 0)
        def _():
            wait(table_ref, table_sems[1])

    table = table_ref[...]
    put_means = pltpu.make_async_copy(
        table_ref.at[pl.ds(pl.multiple_of(4 * rows, 4), 4)], mean_ref, mean_sem
    )
    put_means.start()
    wide = jnp.concatenate([table[0:64], table[64:128]], 1)
    wide = jnp.concatenate(split(wide, 2), 0).astype(BF)
    def look_step(block, _):
        span = 16384 // BLOCKS
        lanes = pl.ds(pl.multiple_of(span * block, span), span)
        found = jnp.dot(wide, low_hot_ref[:, lanes], preferred_element_type=F32)
        for u in range(span // 128):
            row = pl.ds(block * (span // 128) + u, 1)
            at = slice(128 * u, 128 * u + 128)
            part = found[0:64, at] + found[64:128, at]
            own = jnp.broadcast_to(ids_ref[3, row, :], (64, 128)) == iota0(I32, 64, 128)
            row_mean_ref[row, :] = jnp.sum(jnp.where(own, part, 0.0), axis=0, keepdims=True)
        return 0

    with jax.named_scope("look"):
        lax.fori_loop(0, BLOCKS, look_step, 0)
    bound = jnp.max(jnp.max(jnp.abs(table), axis=0, keepdims=True), axis=1, keepdims=True) + 6.0
    left_over = bound * 2.0**60
    scale = jnp.full_like(bound, 2.0**60)
    for step in (64, 32, 16, 8, 4, 2, 1):
        large = left_over >= 2.0**step
        left_over = jnp.where(large, left_over * 2.0**-step, left_over)
        scale = jnp.where(large, scale * 2.0**-step, scale)
    back = jnp.full_like(scale, 2.0**-7) / scale
    scale = scale * 2.0**7
    adjusted = (g_ref[...] + hess * row_mean_ref[...]).astype(BF).astype(F32)
    left_terms(0, adjusted * scale)
    left_rows((0, 1))

    low_half = lax.broadcasted_iota(I32, (8, 128), 1) < BINS

    def histogram(c, first, count):
        with jax.named_scope("mm"):
            start = pl.multiple_of(512 * c + BINS * first, BINS * count)
            hot = hot_ref[pl.ds(start, BINS * count), :]
            both = lax.dot_general(left_ref[...], hot, NT, preferred_element_type=F32)
            grad = (both[0:32] + both[32:64] * 0.0625) * back
            hess = (both[64:96] + both[96:128] * 0.0625) * (1.0 / 128.0)
            for to in range(NY):
                for pair in range(count // 2):
                    a = grad[8 * to : 8 * to + 8, 128 * pair : 128 * pair + 128]
                    b = hess[8 * to : 8 * to + 8, 128 * pair : 128 * pair + 128]
                    f = first + 2 * pair
                    out_y[c, to, f] = jnp.where(low_half, a, pltpu.roll(b, 64, 1))
                    out_y[c, to, f + 1] = jnp.where(low_half, pltpu.roll(a, 64, 1), b)
        at = pl.ds(first, count)
        for k in FAR_Y:
            send(
                out_y.at[c, lax.rem(y + k, NY), at], in_y.at[c, k - 1, at],
                (y_send.at[c], y_recv.at[c]), y_peer(k),
            ).start()

    def second_stage(c):
        with jax.named_scope("ywait"):
            wait_both(in_y.at[c], (y_send.at[c], y_recv.at[c]))
        for f in range(8):
            part = out_y[c, y, f] + in_y[c, 0, f] + in_y[c, 1, f] + in_y[c, 2, f]
            out_z[c, pl.ds(f, 8, stride=8), :] = part
        lines = pl.ds(pl.multiple_of(8 * c, 8), 8)
        for k in FAR_Z:
            at = pl.ds(pl.multiple_of(8 * lax.rem(z + k, NZ), 8), 8)
            send(
                out_z.at[c, at], parts_ref.at[k - 1, lines], (z_send.at[c], z_recv.at[c]), z_peer(k)
            ).start()
        at = pl.ds(pl.multiple_of(8 * z, 8), 8)
        pltpu.make_async_copy(out_z.at[c, at], parts_ref.at[NZ - 1, lines], own_sem).start()

    def chunk(c, _):
        histogram(c, 0, 8)

        @pl.when(c >= 2)
        def _():
            second_stage(c - 2)

        return 0

    def last_chunk(n, _):
        histogram(CHUNKS - 1, 4 * n, 4)
        second_stage(CHUNKS - 3 + n)
        return 0

    lax.fori_loop(0, CHUNKS - 1, chunk, 0)
    lax.fori_loop(0, 2, last_chunk, 0)
    second_stage(CHUNKS - 1)
    with jax.named_scope("zwait"):
        for c in range(CHUNKS):
            wait_both(parts_ref.at[pl.ds(0, NZ - 1), pl.ds(8 * c, 8)], (z_send.at[c], z_recv.at[c]))
        wait(parts_ref.at[NZ - 1], own_sem)
    put_means.wait()


def last_sum(parts_ref, mean_ref, hist_ref, out_ref):
    total = parts_ref[0]
    for k in range(1, NZ):
        total = total + parts_ref[k]
    hist_ref[...] = total
    out_ref[...] = mean_ref[...]


def shards(gradient, hessian, groups, leaf_ids, bins, group_sizes, variance_ratio):
    count = gradient.shape[0]
    vmem, sem = pltpu.VMEM, pltpu.SemaphoreType.DMA
    whole = pl.BlockSpec(memory_space=pltpu.VMEM)
    parts, means = pl.pallas_call(
        kernel,
        out_shape=(jax.ShapeDtypeStruct((NZ, 32, 128), F32), jax.ShapeDtypeStruct((4, 128), F32)),
        in_specs=[pl.BlockSpec(memory_space=pl.ANY)] * 5
        + [pl.BlockSpec(memory_space=pltpu.SMEM), pl.BlockSpec(memory_space=pl.ANY)],
        out_specs=(pl.BlockSpec(memory_space=pl.ANY),) * 2,
        scratch_shapes=[
            vmem((128, 128), F32),
            vmem((128, 128), BF),
            vmem((128, 128), I32),
            vmem((128, 128), I32),
            vmem((4, 128), I32),
            vmem((32, count), I32),
            vmem((32 * BINS, count), F8),
            vmem((4 * LEAVES, count), F8),
            vmem((256, count), BF),
            vmem((5, 128, 128), I32),
            vmem((4, 128, 128), F32),
            vmem((128, 128), F32),
            vmem((32, 128), F32),
            vmem((NY - 1, 32, 128), F32),
            vmem((32, 128), F32),
            vmem((NZ - 1, 32, 128), F32),
            vmem((4, 128), F32),
            vmem((NY - 1, 4, 128), F32),
            vmem((16, 128), F32),
            vmem((32, 128), F32),
            vmem((128, 128), F32),
            vmem((CHUNKS, NY, 8, 8, 128), F32),
            vmem((CHUNKS, NY - 1, 8, 8, 128), F32),
            vmem((CHUNKS, 64, 128), F32),
            sem((6,)), sem, sem,
            sem((5,)), sem((5,)),
            sem((CHUNKS,)), sem((CHUNKS,)), sem((CHUNKS,)), sem((CHUNKS,)),
        ],
        compiler_params=pltpu.CompilerParams(
            collective_id=0, has_side_effects=True, vmem_limit_bytes=56 * 1024 * 1024
        ),
    )(
        gradient.reshape(128, 128),
        hessian.reshape(128, 128),
        groups.reshape(128, 128),
        leaf_ids.reshape(128, 128),
        group_sizes.reshape(4, 128),
        variance_ratio,
        bins,
    )
    hist, means = pl.pallas_call(
        last_sum,
        out_shape=(jax.ShapeDtypeStruct((32, 128), F32), jax.ShapeDtypeStruct((4, 128), F32)),
        in_specs=[whole] * 2,
        out_specs=(whole, whole),
    )(parts, means)
    return hist.reshape(1, 32, 128), means.reshape(512)


def solution(mesh):
    in_specs = (P("rows"), P("rows"), P("rows"), P("rows"), P("feat", "rows"), P("rows"), P())
    out_specs = (P("rows", "feat", None), P("rows"))
    return jax.shard_map(shards, mesh=mesh, in_specs=in_specs, out_specs=out_specs, check_vma=False)
```
